32 devices in a mesh: lat: 4 (over z), lon: 8 (over y, x, core).
Axes of the slice: x: 2, y: 2, z: 4, core: 2. Of those that a mesh axis runs over, the one named last changes fastest.
Arguments:
- latent: bfloat16 [4, 48, 192, 512], P(None, 'lat', 'lon'), may hold values from -6 to 6
- gain_first: float32 [512], replicated, may hold values from 0.25 to 1.75
- triple_first: bfloat16 [512, 1536], replicated, may hold values from -3.75 to 3.75
- output_first: bfloat16 [512, 512], replicated, may hold values from -0.25 to 0.25
- gain_merge: float32 [2048], replicated, may hold values from 0.25 to 1.75
- merge_weight: bfloat16 [2048, 1024], replicated, may hold values from -0.125 to 0.125
- gain_second: float32 [1024], replicated, may hold values from 0.25 to 1.75
- triple_second: bfloat16 [1024, 3072], replicated, may hold values from -2.6516504 to 2.6516504
- output_second: bfloat16 [1024, 1024], replicated, may hold values from -0.1875 to 0.1875
- split_weight: bfloat16 [1024, 2048], replicated, may hold values from -0.1875 to 0.1875
Outputs:
- decoded: bfloat16 [4, 48, 192, 512], P(None, 'lat', 'lon')
- level_means: float32 [4, 512], replicated
The draws below stay inside these ranges and needn't reach their ends.
All inputs are finite; a program needn't handle non-finite values.
Results may differ from the reference program's by a relative error of at most 0.028.
Values may be sent and summed in bfloat16 or wider, within the bound.
No kernel may reach another device: no remote copies, remote signals or barrier semaphores. Data moves between devices by JAX's collectives and lax.ppermute only.
A program may use at most 192 MiB of HBM per device.

```python
import jax
import jax.numpy as jnp
from jax import lax

D1 = 512
D2 = 1024
HD = 64
LEVELS = 4
WIN_LEV = 2
WIN_LAT = 6
WIN_LON = 12
LAT = 48
LON = 192


def triple_draw(key, width):
    spread = (width // 2) ** (-0.5)
    base_key = jax.random.fold_in(jax.random.fold_in(key, 31), 0)
    drawn = jnp.clip(jax.random.normal(base_key, (width, 3 * width), jnp.float32), -6.0, 6.0)
    return (drawn * spread).astype(jnp.bfloat16)


def draw_triple_first(key, part):
    return triple_draw(jax.random.fold_in(key, 3), D1)


def draw_triple_second(key, part):
    return triple_draw(jax.random.fold_in(key, 7), D2)


def steps_of(key, extent, pieces, least, largest):
    loudness = 1.0
    for dim, shards_of in pieces:
        heights = jax.random.uniform(jax.random.fold_in(jax.random.fold_in(key, 6), dim), (shards_of,), jnp.float32, least / len(pieces), largest / len(pieces))
        loudness = loudness * jnp.repeat(jnp.exp(heights), extent[dim] // shards_of).reshape((-1,) + (1,) * (len(extent) - 1 - dim))
    return loudness


def scatter_about(own_key, extent, scale, limit, pieces=(), kind=jnp.bfloat16):
    loudness = steps_of(own_key, extent, pieces, -0.22, 0.18) if pieces else 1.0
    result = jax.random.normal(own_key, extent, jnp.float32) * scale * loudness
    return jnp.minimum(jnp.maximum(result, -limit), limit).astype(kind)


def setup_inputs(seed: int = 0) -> dict:
    seeds = jax.random.split(jax.random.key(seed), 11)
    return {
        "latent": scatter_about(seeds[0], (LEVELS, LAT, LON, D1), 1.0, 6.0, ((1, 4), (2, 8))),
        "gain_first": jnp.clip(1.0 + 0.15 * jax.random.normal(seeds[1], (D1,), jnp.float32), 0.25, 1.75),
        "triple_first": draw_triple_first(jax.random.fold_in(seeds[10], 71), 0),
        "output_first": scatter_about(seeds[3], (D1, D1), D1 ** -0.5, 0.25),
        "gain_merge": jnp.clip(1.0 + 0.15 * jax.random.normal(seeds[4], (4 * D1,), jnp.float32), 0.25, 1.75),
        "merge_weight": scatter_about(seeds[5], (4 * D1, D2), (4 * D1) ** -0.5, 0.125),
        "gain_second": jnp.clip(1.0 + 0.15 * jax.random.normal(seeds[6], (D2,), jnp.float32), 0.25, 1.75),
        "triple_second": draw_triple_second(jax.random.fold_in(seeds[10], 71), 0),
        "output_second": scatter_about(seeds[8], (D2, D2), D2 ** -0.5, 0.1875),
        "split_weight": scatter_about(seeds[9], (D2, 4 * D1), D2 ** -0.5, 0.1875),
    }


epsilon = 1e-05
masked_score = -1e+30

def layer_norm(values_in, norm_gain):
    row_mean = lax.optimization_barrier(jnp.mean(values_in, -1, keepdims=True))
    centred = values_in - row_mean
    row_var = lax.optimization_barrier(jnp.mean(centred * centred, -1, keepdims=True))
    return centred * lax.rsqrt(row_var + epsilon) * norm_gain.astype(jnp.float32)

def level_windows(levels):
    half_lev = WIN_LEV // 2
    level_index = (jnp.arange(levels, dtype=jnp.int32) + half_lev) % levels
    return (level_index + half_lev) // WIN_LEV

def window_block(field_tile, level_ids, row_ids, row_valid, norm_gain, w_proj, w_out, top_row, left_col, keep_rows, keep_cols):
    levels, height, tile_cols, channels = field_tile.shape
    head_count = channels // HD
    lev_wins = levels // WIN_LEV
    win_rows = height // WIN_LAT
    win_cols = tile_cols // WIN_LON
    window_count = lev_wins * win_rows * win_cols
    normed = layer_norm(field_tile.astype(jnp.float32), norm_gain).astype(jnp.bfloat16)
    projected = jnp.dot(normed.reshape(-1, channels), w_proj, preferred_element_type=jnp.float32).astype(jnp.bfloat16)
    projected = projected.reshape(lev_wins, WIN_LEV, win_rows, WIN_LAT, win_cols, WIN_LON, 3, head_count, HD)
    projected = jnp.transpose(projected, (6, 0, 2, 4, 7, 1, 3, 5, 8))
    projected = projected.reshape(3, window_count, head_count, WIN_LEV * WIN_LAT * WIN_LON, HD)
    queries = projected[0].astype(jnp.float32)
    key_rows = projected[1].astype(jnp.float32)
    values = projected[2].astype(jnp.float32)
    scores = jnp.einsum('wgqd,wgkd->wgqk', queries, key_rows) * HD ** (-0.5)
    shape_ids = (lev_wins, win_rows, win_cols, WIN_LEV, WIN_LAT, WIN_LON)
    token_rows = jnp.broadcast_to(row_ids.reshape(1, win_rows, 1, 1, WIN_LAT, 1), shape_ids).reshape(window_count, -1)
    token_valid = jnp.broadcast_to(row_valid.reshape(1, win_rows, 1, 1, WIN_LAT, 1), shape_ids).reshape(window_count, -1)
    token_levels = jnp.broadcast_to(level_ids.reshape(lev_wins, 1, 1, WIN_LEV, 1, 1), shape_ids).reshape(window_count, -1)
    allowed = (token_rows[:, :, None] == token_rows[:, None, :]) & (token_levels[:, :, None] == token_levels[:, None, :]) & token_valid[:, None, :]
    scores = jnp.where(allowed[:, None], scores, masked_score)
    row_peak = lax.optimization_barrier(jnp.max(scores, -1, keepdims=True))
    exponent = jnp.exp(scores - row_peak)
    row_total = lax.optimization_barrier(jnp.sum(exponent, -1, keepdims=True))
    weights = (exponent / row_total).astype(jnp.bfloat16)
    attended = jnp.einsum('wgqk,wgkd->wgqd', weights.astype(jnp.float32), values).astype(jnp.bfloat16)
    attended = attended.reshape(lev_wins, win_rows, win_cols, head_count, WIN_LEV, WIN_LAT, WIN_LON, HD)
    attended = jnp.transpose(attended, (0, 4, 1, 5, 2, 6, 3, 7)).reshape(levels, height, tile_cols, channels)
    attended = attended[:, top_row:top_row + keep_rows, left_col:left_col + keep_cols]
    update = jnp.dot(attended.reshape(-1, channels), w_out, preferred_element_type=jnp.float32)
    update = update.reshape(levels, keep_rows, keep_cols, channels)
    base_rows = field_tile[:, top_row:top_row + keep_rows, left_col:left_col + keep_cols].astype(jnp.float32)
    return (base_rows + update).astype(jnp.bfloat16)

def shifted_section(field, norm_gain, w_proj, w_out):
    levels, height, tile_cols, channels = field.shape
    half_lev = WIN_LEV // 2
    half_lat = WIN_LAT // 2
    half_lon = WIN_LON // 2
    rolled = jnp.roll(field, (-half_lev, -half_lat, -half_lon), (0, 1, 2))
    band_count = height // WIN_LAT
    stacked = jnp.transpose(rolled.reshape(levels, band_count, WIN_LAT, tile_cols, channels), (1, 0, 2, 3, 4))
    band_starts = jnp.arange(band_count, dtype=jnp.int32) * WIN_LAT
    level_ids = level_windows(levels)

    def one_band(band_args):
        band_field, band_start = band_args
        row_index = (band_start + half_lat + jnp.arange(WIN_LAT, dtype=jnp.int32)) % height
        row_ids = (row_index + half_lat) // WIN_LAT
        row_valid = jnp.ones((WIN_LAT,), bool)
        return window_block(band_field, level_ids, row_ids, row_valid, norm_gain, w_proj, w_out, 0, 0, WIN_LAT, tile_cols)
    banded = lax.map(one_band, (stacked, band_starts))
    banded = jnp.transpose(banded, (1, 0, 2, 3, 4)).reshape(levels, height, tile_cols, channels)
    return jnp.roll(banded, (half_lev, half_lat, half_lon), (0, 1, 2))

def merge_patches(field, norm_gain, w_merge):
    levels, height, tile_cols, channels = field.shape
    grouped = field.reshape(levels, height // 2, 2, tile_cols // 2, 2, channels)
    grouped = jnp.transpose(grouped, (0, 1, 3, 2, 4, 5)).reshape(levels, height // 2, tile_cols // 2, 4 * channels)
    normed = layer_norm(grouped.astype(jnp.float32), norm_gain).astype(jnp.bfloat16)
    merged = jnp.dot(normed.reshape(-1, 4 * channels), w_merge, preferred_element_type=jnp.float32).astype(jnp.bfloat16)
    return merged.reshape(levels, height // 2, tile_cols // 2, -1)

def split_patches(coarse, skip_field, w_split):
    levels, half_rows, half_cols, wide = coarse.shape
    channels = skip_field.shape[-1]
    spread = jnp.dot(coarse.reshape(-1, wide), w_split, preferred_element_type=jnp.float32)
    spread = spread.reshape(levels, half_rows, half_cols, 2, 2, channels)
    spread = jnp.transpose(spread, (0, 1, 3, 2, 4, 5)).reshape(levels, 2 * half_rows, 2 * half_cols, channels)
    return (skip_field.astype(jnp.float32) + spread).astype(jnp.bfloat16)

def row_weights(row_index, total_rows):
    position = (row_index.astype(jnp.float32) + 0.5) / total_rows - 0.5
    return jnp.cos(jnp.pi * position)

def reference(latent, gain_first, triple_first, output_first, gain_merge, merge_weight, gain_second, triple_second, output_second, split_weight):
    fine_field = shifted_section(latent, gain_first, triple_first, output_first)
    coarse = merge_patches(fine_field, gain_merge, merge_weight)
    upper = shifted_section(coarse, gain_second, triple_second, output_second)
    decoded = split_patches(upper, fine_field, split_weight)
    total_rows = decoded.shape[1]
    all_weights = row_weights(jnp.arange(total_rows, dtype=jnp.int32), total_rows)
    scale_total = jnp.sqrt(decoded.shape[2] * jnp.sum(all_weights * all_weights))
    summed = lax.optimization_barrier(jnp.sum(decoded.astype(jnp.float32) * all_weights[None, :, None, None], (1, 2)))
    return (decoded, summed / scale_total)
```

```python
import functools
import math

import jax
import jax.numpy as jnp
import numpy as np
from jax import lax
from jax.experimental import pallas as pl
from jax.experimental.pallas import tpu as pltpu
from jax.sharding import PartitionSpec as P

HD = 64
WIN_LEV = 2
WIN_LAT = 6
WIN_LON = 12
HALF_LAT = WIN_LAT // 2
HALF_LON = WIN_LON // 2
LANES = 128

epsilon = 1e-05
masked_score = -1e30
score_scale = HD**-0.5 * math.log2(math.e)


class Plan:
    def __init__(self, levels, height, width):
        self.levels, self.height, self.width = levels, height, width
        assert levels % WIN_LEV == 0
        assert height == 2 * WIN_LAT and width == 2 * WIN_LON
        self.groups = levels // WIN_LEV
        half_lev = WIN_LEV // 2
        self.group_levels = [
            [(g * WIN_LEV + half_lev + i) % levels for i in range(WIN_LEV)] for g in range(self.groups)
        ]
        self.order = [lv for group in self.group_levels for lv in group]
        ids = [(((lv + half_lev)) // WIN_LEV) for lv in range(levels)]
        self.group_split = [len({ids[lv] for lv in group}) > 1 for group in self.group_levels]
        self.window = WIN_LEV * WIN_LAT * WIN_LON
        self.windows = [(wr, wc) for wr in range(height // WIN_LAT) for wc in range(width // WIN_LON)]

        own = [(lv, r, c) for lv in range(levels) for r in range(height) for c in range(width)]

        def boxed(rows, cols):
            return [(lv, r, c) for lv in self.order for r in range(*rows) for c in range(*cols)]

        def frame(windows, g):
            return [
                (lv, HALF_LAT + wr * WIN_LAT + r, HALF_LON + wc * WIN_LON + c)
                for wr, wc in windows
                for lv in self.group_levels[g]
                for r in range(WIN_LAT)
                for c in range(WIN_LON)
            ]

        self.own = own
        self.first = sum([frame(self.windows[:1], g) for g in range(self.groups)], [])
        self.rest = sum([frame(self.windows[1:], g) for g in range(self.groups)], [])
        fl, fc, fh, fw = HALF_LAT, HALF_LON, height, width
        self.raw_lat = boxed((fh, fh + fl), (fc, fw))
        self.raw_lon = boxed((fl, fh), (fw, fw + fc))
        self.raw_diag = boxed((fh, fh + fl), (fw, fw + fc))
        self.res_lat = boxed((fh + fl, fh + 2 * fl), (2 * fc, fw + fc))
        self.res_lon = boxed((2 * fl, fh + fl), (fw + fc, fw + 2 * fc))
        self.res_diag = boxed((fh + fl, fh + 2 * fl), (fw + fc, fw + 2 * fc))
        self.coarse_rows, self.coarse_cols = height // 2, width // 2
        self.parts = [
            [
                (lv, 2 * fl + 2 * r + ro, 2 * fc + 2 * c + co)
                for lv in self.order
                for r in range(self.coarse_rows)
                for c in range(self.coarse_cols)
            ]
            for ro in range(2)
            for co in range(2)
        ]

    def shifted(self, cells, rows, cols):
        return [(lv, r - rows, c - cols) for lv, r, c in cells]


def scatter_map(source, target):
    place = {cell: i for i, cell in enumerate(target)}
    assert len(place) == len(target)
    return np.array([place.get(cell, -1) for cell in source], np.int32)


class Maps:
    def __init__(self):
        self.rows = []

    def add(self, vector):
        self.rows.append(vector)
        return (len(self.rows) - 1, len(vector))

    def array(self):
        width = -(-max(len(v) for v in self.rows) // LANES) * LANES
        height = -(-len(self.rows) // 8) * 8
        out = np.full((height, width), -1, np.int32)
        for i, v in enumerate(self.rows):
            out[i, : len(v)] = v
        return jnp.asarray(out)


def picked(maps_ref, key, out_rows, source, offset=0):
    row, count = key
    index = maps_ref[row : row + 1, :count]
    hot = lax.broadcasted_iota(jnp.int32, (out_rows, count), 0) + offset == index
    return jnp.dot(
        jnp.where(hot, 1.0, 0.0).astype(jnp.bfloat16), source, preferred_element_type=jnp.float32
    )


def normed_rows(value, gain):
    mean = jnp.mean(value, -1, keepdims=True)
    centred = value - mean
    var = jnp.mean(centred * centred, -1, keepdims=True)
    return (centred * lax.rsqrt(var + epsilon) * gain).astype(jnp.bfloat16)


def score_bias(count, group_split, edge):
    span = count // WIN_LEV
    rows = lax.broadcasted_iota(jnp.int32, (count, count), 0)
    cols = lax.broadcasted_iota(jnp.int32, (count, count), 1)
    q_lev, k_lev = rows >= span, cols >= span
    q_in = rows - jnp.where(q_lev, span, 0)
    k_in = cols - jnp.where(k_lev, span, 0)
    half = span // 2
    apart = ((q_in >= half) != (k_in >= half)) & edge
    if group_split:
        apart = apart | (q_lev != k_lev)
    return jnp.where(apart, masked_score, 0.0)


def head_pair(q, k, v, bias, low, high):
    trans = (((1,), (1,)), ((), ()))
    outs = []
    for keep, fill in ((low, high), (high, low)):
        s = lax.dot_general(q, k * keep, trans, preferred_element_type=jnp.float32)
        if bias is not None:
            s = s + bias
        peak = jnp.max(s, -1, keepdims=True)
        p = jnp.exp2((s - peak) * score_scale).astype(jnp.bfloat16)
        outs.append(jnp.dot(p, v * keep + fill, preferred_element_type=jnp.float32))
    is_low = lax.broadcasted_iota(jnp.int32, outs[0].shape, 1) < HD
    top = jnp.where(is_low, outs[0], outs[1])
    bottom = pltpu.roll(jnp.where(is_low, outs[1], outs[0]), HD, 1)
    return (top / bottom).astype(jnp.bfloat16)


def lane_masks():
    lane = lax.broadcasted_iota(jnp.int32, (1, LANES), 1)
    low = jnp.where(lane < HD, 1.0, 0.0).astype(jnp.bfloat16)
    high = jnp.where(lane < HD, 0.0, 1.0).astype(jnp.bfloat16)
    return low, high


def block_attention(qkv, att, row, channels, pair, bias, count):
    low, high = lane_masks()
    rows = pl.ds(row, count)
    base = pair * LANES

    def lanes(offset):
        return pl.ds(pl.multiple_of(base + offset, LANES), LANES)

    q = qkv[rows, lanes(0)]
    k = qkv[rows, lanes(channels)]
    v = qkv[rows, lanes(2 * channels)]
    att[rows, lanes(0)] = head_pair(q, k, v, bias, low, high)


def pack_kernel(plan_keys, maps_ref, x_ref, lat_ref, lon_ref, diag_ref):
    x = x_ref[...]
    for key, out in zip(plan_keys, (lat_ref, lon_ref, diag_ref)):
        out[...] = picked(maps_ref, key, out.shape[0], x).astype(jnp.bfloat16)


def fine_first_kernel(plan, keys, maps_ref, x_ref, gain_ref, w_ref, wo_ref, y_ref, rest_ref, qkv, att, bias):
    channels = x_ref.shape[1]
    x = x_ref[...]
    count = plan.window
    tokens = picked(maps_ref, keys["first"], y_ref.shape[0], x)
    normed = normed_rows(tokens, gain_ref[...])
    qkv[...] = jnp.dot(normed, w_ref[...], preferred_element_type=jnp.float32).astype(jnp.bfloat16)
    rest_ref[...] = picked(maps_ref, keys["rest"], rest_ref.shape[0], x).astype(jnp.bfloat16)
    never = jnp.zeros((count, count), jnp.int32) > 0
    for g in range(plan.groups):
        bias[g] = score_bias(count, plan.group_split[g], never)

    @pl.loop(0, channels // LANES)
    def _(pair):
        for g in range(plan.groups):
            b = bias[g] if plan.group_split[g] else None
            block_attention(qkv, att, g * count, channels, pair, b, count)

    update = jnp.dot(att[...], wo_ref[...], preferred_element_type=jnp.float32)
    y_ref[...] = (tokens + update).astype(jnp.bfloat16)


def fine_rest_kernel(
    plan, keys, maps_ref, edge_ref, first_ref, rest_ref, lat_ref, lon_ref, diag_ref, gain_ref, w_ref, wo_ref,
    y_ref, slat_ref, slon_ref, sdiag_ref, qkv, att, bias,
):
    channels = rest_ref.shape[1]
    count = plan.window
    total = rest_ref.shape[0]
    tokens = rest_ref[...].astype(jnp.float32)
    for key, ref in (("raw_lat", lat_ref), ("raw_lon", lon_ref), ("raw_diag", diag_ref)):
        tokens = tokens + picked(maps_ref, keys[key], total, ref[...])
    normed = normed_rows(tokens, gain_ref[...])
    qkv[...] = jnp.dot(normed, w_ref[...], preferred_element_type=jnp.float32).astype(jnp.bfloat16)
    edge = jnp.full((count, count), edge_ref[0], jnp.int32) > 0
    never = jnp.zeros((count, count), jnp.int32) > 0
    for g in range(plan.groups):
        bias[2 * g] = score_bias(count, plan.group_split[g], never)
        bias[2 * g + 1] = score_bias(count, plan.group_split[g], edge)
    spread = len(plan.windows) - 1
    pairs = channels // LANES

    @pl.loop(0, pairs * spread)
    def _(step):
        pair = step % pairs
        w = step // pairs
        below = jnp.where(w + 1 >= plan.width // WIN_LON, 1, 0)
        for g in range(plan.groups):
            row = pl.multiple_of((g * spread + w) * count, 16)
            block_attention(qkv, att, row, channels, pair, bias[2 * g + below], count)

    update = jnp.dot(att[...], wo_ref[...], preferred_element_type=jnp.float32)
    y = (tokens + update).astype(jnp.bfloat16)
    y_ref[...] = y
    first = first_ref[...]
    for name, out in (("res_lat", slat_ref), ("res_lon", slon_ref), ("res_diag", sdiag_ref)):
        value = picked(maps_ref, keys[name, "first"], out.shape[0], first)
        if (name, "rest") in keys:
            value = value + picked(maps_ref, keys[name, "rest"], out.shape[0], y)
        out[...] = value.astype(jnp.bfloat16)


def coarse_own_kernel(plan, keys, maps_ref, first_ref, rest_ref, part_ref):
    first = first_ref[...]
    rest = rest_ref[...]
    total = part_ref.shape[1]
    for k in range(len(plan.parts)):
        value = picked(maps_ref, keys["part", k, "first"], total, first)
        value = value + picked(maps_ref, keys["part", k, "rest"], total, rest)
        part_ref[k] = value.astype(jnp.bfloat16)


def coarse_kernel(
    plan, keys, maps_ref, edge_ref, part_ref, lat_ref, lon_ref, diag_ref, gm_ref, wm_ref, gs_ref, ws_ref, wo_ref,
    wsp_ref, weight_ref, own_ref, slat_ref, slon_ref, sdiag_ref, sums_ref, fine, qkv, att, bias, decoded,
):
    parts = len(plan.parts)
    total, channels = part_ref.shape[1:]
    wide = ws_ref.shape[0]
    count = plan.window
    sums = 0.0
    for k in range(parts):
        value = part_ref[k].astype(jnp.float32)
        for name, ref in (("res_lat", lat_ref), ("res_lon", lon_ref), ("res_diag", diag_ref)):
            if ("part", k, name) in keys:
                value = value + picked(maps_ref, keys["part", k, name], total, ref[...])
        fine[k] = value
        sums = sums + jnp.sum(value, -1, keepdims=True)
    mean = sums / (parts * channels)
    square = 0.0
    for k in range(parts):
        centred = fine[k] - mean
        square = square + jnp.sum(centred * centred, -1, keepdims=True)
    scale = lax.rsqrt(square / (parts * channels) + epsilon)
    merged = 0.0
    for k in range(parts):
        span = slice(k * channels, (k + 1) * channels)
        normed = ((fine[k] - mean) * scale * gm_ref[:, span]).astype(jnp.bfloat16)
        merged = merged + jnp.dot(normed, wm_ref[span, :], preferred_element_type=jnp.float32)
    coarse = merged.astype(jnp.bfloat16).astype(jnp.float32)
    normed = normed_rows(coarse, gs_ref[...])
    qkv[...] = jnp.dot(normed, ws_ref[...], preferred_element_type=jnp.float32).astype(jnp.bfloat16)
    edge = jnp.full((count, count), edge_ref[0], jnp.int32) > 0
    for g in range(plan.groups):
        bias[g] = score_bias(count, plan.group_split[g], edge)

    @pl.loop(0, wide // LANES)
    def _(pair):
        for g in range(plan.groups):
            block_attention(qkv, att, g * count, wide, pair, bias[g], count)

    update = jnp.dot(att[...], wo_ref[...], preferred_element_type=jnp.float32)
    upper = (coarse + update).astype(jnp.bfloat16)
    levels = plan.levels
    span = total // levels
    for k in range(parts):
        spread = jnp.dot(upper, wsp_ref[:, k * channels : (k + 1) * channels], preferred_element_type=jnp.float32)
        value = (fine[k] + spread).astype(jnp.bfloat16)
        wide_value = value.astype(jnp.float32)
        weighted = wide_value * weight_ref[k]
        for i, lv in enumerate(plan.order):
            part = jnp.sum(weighted[i * span : (i + 1) * span], 0, keepdims=True)
            if k == 0:
                sums_ref[lv : lv + 1, :] = part
            else:
                sums_ref[lv : lv + 1, :] += part
        decoded[k] = wide_value
    quarter = parts * (span // 4)
    for i in range(levels):
        stacked = jnp.concatenate([decoded[k, i * span : (i + 1) * span] for k in range(parts)], 0)
        moved = picked(maps_ref, keys["quarters"], parts * span, stacked.astype(jnp.bfloat16)).astype(jnp.bfloat16)
        for q, out in enumerate((own_ref, slon_ref, slat_ref, sdiag_ref)):
            out[i * quarter : (i + 1) * quarter, :] = moved[q * quarter : (q + 1) * quarter]


def output_kernel(plan, keys, maps_ref, own_ref, lon_ref, lat_ref, diag_ref, out_ref):
    span = own_ref.shape[0] // plan.levels
    tile = plan.height * plan.width
    for i, lv in enumerate(plan.order):
        rows = slice(i * span, (i + 1) * span)
        stacked = jnp.concatenate(
            [ref[rows, :].astype(jnp.float32) for ref in (own_ref, lon_ref, lat_ref, diag_ref)], 0
        ).astype(jnp.bfloat16)
        out_ref[lv * tile : (lv + 1) * tile, :] = picked(maps_ref, keys["output"], tile, stacked).astype(jnp.bfloat16)


def all_summed(value, axes):
    for axis in axes:
        count = lax.axis_size(axis)
        if count & (count - 1):
            value = lax.psum(value, axis)
            continue
        step = 1
        while step < count:
            value = value + lax.ppermute(value, axis, [(i, i ^ step) for i in range(count)])
            step *= 2
    return value


def shards(
    latent, gain_first, triple_first, output_first, gain_merge, merge_weight, gain_second, triple_second,
    output_second, split_weight,
):
    levels, height, width, channels = latent.shape
    wide = merge_weight.shape[1]
    plan = Plan(levels, height, width)
    maps = Maps()
    lat_count, lon_count = lax.axis_size("lat"), lax.axis_size("lon")

    def moved(value, lat_step, lon_step):
        pairs = [
            (a * lon_count + b, (a + lat_step) % lat_count * lon_count + (b + lon_step) % lon_count)
            for a in range(lat_count)
            for b in range(lon_count)
        ]
        return lax.ppermute(value, ("lat", "lon"), pairs)

    pack_keys = (
        maps.add(scatter_map(plan.own, plan.shifted(plan.raw_lat, height, 0))),
        maps.add(scatter_map(plan.own, plan.shifted(plan.raw_lon, 0, width))),
        maps.add(scatter_map(plan.own, plan.shifted(plan.raw_diag, height, width))),
    )
    keys = {
        "first": maps.add(scatter_map(plan.own, plan.first)),
        "rest": maps.add(scatter_map(plan.own, plan.rest)),
        "raw_lat": maps.add(scatter_map(plan.raw_lat, plan.rest)),
        "raw_lon": maps.add(scatter_map(plan.raw_lon, plan.rest)),
        "raw_diag": maps.add(scatter_map(plan.raw_diag, plan.rest)),
    }
    results = {
        "res_lat": (plan.res_lat, height, 0),
        "res_lon": (plan.res_lon, 0, width),
        "res_diag": (plan.res_diag, height, width),
    }
    for name, (cells, rows, cols) in results.items():
        sent = plan.shifted(cells, rows, cols)
        for source_name, source in (("first", plan.first), ("rest", plan.rest)):
            vector = scatter_map(source, sent)
            if (vector >= 0).any():
                keys[name, source_name] = maps.add(vector)
        assert (name, "first") in keys
    for k, part in enumerate(plan.parts):
        for name, source in (("first", plan.first), ("rest", plan.rest)):
            keys["part", k, name] = maps.add(scatter_map(source, part))
        for name, (cells, _, _) in results.items():
            vector = scatter_map(cells, part)
            if (vector >= 0).any():
                keys["part", k, name] = maps.add(vector)
    cells = [
        (2 * r + ro, 2 * c + co)
        for ro in range(2)
        for co in range(2)
        for r in range(plan.coarse_rows)
        for c in range(plan.coarse_cols)
    ]
    half_rows, half_cols = height // 2, width // 2
    quarters = [
        (qr * half_rows + r, qc * half_cols + c)
        for qr in range(2)
        for qc in range(2)
        for r in range(half_rows)
        for c in range(half_cols)
    ]
    keys["quarters"] = maps.add(scatter_map(cells, quarters))
    placed = [((r + half_rows) % height, (c + half_cols) % width) for r, c in quarters]
    keys["output"] = maps.add(scatter_map(placed, [(r, c) for r in range(height) for c in range(width)]))
    table = maps.array()

    vmem = pl.BlockSpec(memory_space=pltpu.VMEM)
    smem = pl.BlockSpec(memory_space=pltpu.SMEM)
    bf16 = jnp.bfloat16

    def call(body, name, outs, args, scratch=(), scalars=0, flops=0, limit=40):
        size = sum(math.prod(a.shape) * a.dtype.itemsize for a in args)
        return pl.pallas_call(
            body,
            name=name,
            out_shape=[jax.ShapeDtypeStruct(s, d) for s, d in outs],
            in_specs=[smem if a.ndim == 1 else vmem for a in args],
            out_specs=[vmem] * len(outs),
            scratch_shapes=list(scratch),
            cost_estimate=pl.CostEstimate(flops=flops, bytes_accessed=size, transcendentals=0),
            compiler_params=pltpu.CompilerParams(vmem_limit_bytes=limit << 20),
        )(*args)

    count = plan.window
    x = latent.reshape(levels * height * width, channels)
    edge = (lax.axis_index("lat") == lat_count - 1).astype(jnp.int32).reshape(1)
    n_first, n_rest, n_coarse = len(plan.first), len(plan.rest), len(plan.parts[0])
    n_part = len(plan.parts)

    s_lat, s_lon, s_diag = call(
        functools.partial(pack_kernel, pack_keys), "pack",
        [((len(c), channels), bf16) for c in (plan.raw_lat, plan.raw_lon, plan.raw_diag)], (table, x),
        flops=10**9,
    )
    r_lat, r_lon, r_diag = moved(s_lat, -1, 0), moved(s_lon, 0, -1), moved(s_diag, -1, -1)
    gain1 = gain_first.reshape(1, channels)
    y_first, x_rest = call(
        functools.partial(fine_first_kernel, plan, keys), "fine_first",
        [((n_first, channels), bf16), ((n_rest, channels), bf16)],
        (table, x, gain1, triple_first, output_first),
        [
            pltpu.VMEM((n_first, 3 * channels), bf16),
            pltpu.VMEM((n_first, channels), bf16),
            pltpu.VMEM((plan.groups, count, count), jnp.float32),
        ],
        flops=4 * 10**9,
    )
    y_rest, s_lat, s_lon, s_diag = call(
        functools.partial(fine_rest_kernel, plan, keys), "fine_rest",
        [((n_rest, channels), bf16)]
        + [((len(c), channels), bf16) for c in (plan.res_lat, plan.res_lon, plan.res_diag)],
        (table, edge, y_first, x_rest, r_lat, r_lon, r_diag, gain1, triple_first, output_first),
        [
            pltpu.VMEM((n_rest, 3 * channels), bf16),
            pltpu.VMEM((n_rest, channels), bf16),
            pltpu.VMEM((2 * plan.groups, count, count), jnp.float32),
        ],
        flops=6 * 10**9,
    )
    r_lat, r_lon, r_diag = moved(s_lat, -1, 0), moved(s_lon, 0, -1), moved(s_diag, -1, -1)
    (parts,) = call(
        functools.partial(coarse_own_kernel, plan, keys), "coarse_own",
        [((n_part, n_coarse, channels), bf16)], (table, y_first, y_rest), flops=4 * 10**9,
    )
    total_rows = height * lat_count
    total_cols = width * lon_count

    def row_weights(rows):
        return jnp.cos(jnp.pi * ((rows.astype(jnp.float32) + 0.5) / total_rows - 0.5))

    every = row_weights(jnp.arange(total_rows, dtype=jnp.int32))
    scale_total = jnp.sqrt(total_cols * jnp.sum(every * every))
    frame_rows = np.array([[r for _, r, _ in part] for part in plan.parts], np.int32)
    weights = row_weights((lax.axis_index("lat") * height + frame_rows) % total_rows) / scale_total
    own, s_lat, s_lon, s_diag, sums = call(
        functools.partial(coarse_kernel, plan, keys), "coarse",
        [((n_coarse, channels), bf16)] * 4 + [((levels, channels), jnp.float32)],
        (
            table, edge, parts, r_lat, r_lon, r_diag, gain_merge.reshape(1, -1), merge_weight,
            gain_second.reshape(1, -1), triple_second, output_second, split_weight, weights[:, :, None],
        ),
        [
            pltpu.VMEM((n_part, n_coarse, channels), jnp.float32),
            pltpu.VMEM((n_coarse, 3 * wide), bf16),
            pltpu.VMEM((n_coarse, wide), bf16),
            pltpu.VMEM((plan.groups, count, count), jnp.float32),
            pltpu.VMEM((n_part, n_coarse, channels), jnp.float32),
        ],
        flops=8 * 10**9,
    )
    d_lat, d_lon, d_diag = moved(s_lat, 1, 0), moved(s_lon, 0, 1), moved(s_diag, 1, 1)
    means = all_summed(sums, ("lon", "lat"))
    (decoded,) = call(
        functools.partial(output_kernel, plan, keys), "output",
        [((levels * height * width, channels), bf16)], (table, own, d_lon, d_lat, d_diag), flops=10**9,
    )
    return decoded.reshape(latent.shape), means


def solution(mesh):
    return jax.shard_map(
        shards,
        mesh=mesh,
        in_specs=(P(None, "lat", "lon", None), P(), P(), P(), P(), P(), P(), P(), P(), P()),
        out_specs=(P(None, "lat", "lon", None), P()),
        check_vma=False,
    )
```

```python
import functools
import math

import jax
import jax.numpy as jnp
import numpy as np
from jax import lax
from jax.experimental import pallas as pl
from jax.experimental.pallas import tpu as pltpu
from jax.sharding import PartitionSpec as P

HD = 64
WIN_LEV = 2
WIN_LAT = 6
WIN_LON = 12
HALF_LAT = WIN_LAT // 2
HALF_LON = WIN_LON // 2
LANES = 128

epsilon = 1e-05
masked_score = -1e30
score_scale = HD**-0.5 * math.log2(math.e)

LIMITS = {"pack": 60, "first": 16, "rest": 20, "own": 8, "coarse": 16, "split": 8, "output": 8}


class Plan:
    def __init__(self, levels, height, width):
        self.levels, self.height, self.width = levels, height, width
        assert levels % WIN_LEV == 0
        assert height == 2 * WIN_LAT and width == 2 * WIN_LON
        self.groups = levels // WIN_LEV
        half_lev = WIN_LEV // 2
        self.group_levels = [
            [(g * WIN_LEV + half_lev + i) % levels for i in range(WIN_LEV)] for g in range(self.groups)
        ]
        self.order = [lv for group in self.group_levels for lv in group]
        ids = [(((lv + half_lev)) // WIN_LEV) for lv in range(levels)]
        self.group_split = [len({ids[lv] for lv in group}) > 1 for group in self.group_levels]
        self.window = WIN_LEV * WIN_LAT * WIN_LON
        self.windows = [(wr, wc) for wr in range(height // WIN_LAT) for wc in range(width // WIN_LON)]

        own = [(lv, r, c) for lv in range(levels) for r in range(height) for c in range(width)]

        def boxed(rows, cols):
            return [(lv, r, c) for lv in self.order for r in range(*rows) for c in range(*cols)]

        def frame(windows, g):
            return [
                (lv, HALF_LAT + wr * WIN_LAT + r, HALF_LON + wc * WIN_LON + c)
                for wr, wc in windows
                for lv in self.group_levels[g]
                for r in range(WIN_LAT)
                for c in range(WIN_LON)
            ]

        self.own = own
        self.blocks = [sum([frame([w], g) for g in range(self.groups)], []) for w in self.windows]
        self.first = self.blocks[0]
        self.rest = sum(self.blocks[1:], [])
        fl, fc, fh, fw = HALF_LAT, HALF_LON, height, width
        self.raw_lat = boxed((fh, fh + fl), (fc, fw))
        self.raw_lon = boxed((fl, fh), (fw, fw + fc))
        self.raw_diag = boxed((fh, fh + fl), (fw, fw + fc))
        self.res_lat = boxed((fh + fl, fh + 2 * fl), (2 * fc, fw + fc))
        self.res_lon = boxed((2 * fl, fh + fl), (fw + fc, fw + 2 * fc))
        self.res_diag = boxed((fh + fl, fh + 2 * fl), (fw + fc, fw + 2 * fc))
        self.coarse_rows, self.coarse_cols = height // 2, width // 2
        self.parts = [
            [
                (lv, 2 * fl + 2 * r + ro, 2 * fc + 2 * c + co)
                for lv in self.order
                for r in range(self.coarse_rows)
                for c in range(self.coarse_cols)
            ]
            for ro in range(2)
            for co in range(2)
        ]

    def shifted(self, cells, rows, cols):
        return [(lv, r - rows, c - cols) for lv, r, c in cells]


def scatter_map(source, target):
    place = {cell: i for i, cell in enumerate(target)}
    assert len(place) == len(target)
    return np.array([place.get(cell, -1) for cell in source], np.int32)


class Maps:
    def __init__(self):
        self.rows = []

    def add(self, vector):
        self.rows.append(vector)
        return (len(self.rows) - 1, len(vector))

    def array(self):
        width = -(-max(len(v) for v in self.rows) // LANES) * LANES
        height = -(-len(self.rows) // 8) * 8
        out = np.full((height, width), -1, np.int32)
        for i, v in enumerate(self.rows):
            out[i, : len(v)] = v
        return jnp.asarray(out)


def one_hot(maps_ref, key, out_rows):
    row, count = key
    index = maps_ref[row : row + 1, :count]
    hot = lax.broadcasted_iota(jnp.int32, (out_rows, count), 0) == index
    return jnp.where(hot, 1.0, 0.0).astype(jnp.bfloat16)


def picked(maps_ref, key, out_rows, source):
    return jnp.dot(one_hot(maps_ref, key, out_rows), source, preferred_element_type=jnp.float32)


def normed_rows(value, gain):
    mean = jnp.mean(value, -1, keepdims=True)
    centred = value - mean
    var = jnp.mean(centred * centred, -1, keepdims=True)
    return (centred * lax.rsqrt(var + epsilon) * gain).astype(jnp.bfloat16)


def score_bias(count, group_split, edge):
    span = count // WIN_LEV
    rows = lax.broadcasted_iota(jnp.int32, (count, count), 0)
    cols = lax.broadcasted_iota(jnp.int32, (count, count), 1)
    q_lev, k_lev = rows >= span, cols >= span
    q_in = rows - jnp.where(q_lev, span, 0)
    k_in = cols - jnp.where(k_lev, span, 0)
    half = span // 2
    apart = (q_in >= half) != (k_in >= half)
    apart = jnp.where(apart, edge, 0)
    if group_split:
        apart = jnp.where(q_lev != k_lev, 1, apart)
    return jnp.where(apart > 0, masked_score, 0.0)


def head_pair(q, k, v, bias, low, high):
    trans = (((1,), (1,)), ((), ()))
    outs = []
    for keep, fill in ((low, high), (high, low)):
        s = lax.dot_general(q, k * keep, trans, preferred_element_type=jnp.float32)
        if bias is not None:
            s = s + bias
        peak = jnp.max(s, -1, keepdims=True)
        p = jnp.exp2((s - peak) * score_scale).astype(jnp.bfloat16)
        outs.append(jnp.dot(p, v * keep + fill, preferred_element_type=jnp.float32))
    is_low = lax.broadcasted_iota(jnp.int32, outs[0].shape, 1) < HD
    top = jnp.where(is_low, outs[0], outs[1])
    bottom = pltpu.roll(jnp.where(is_low, outs[1], outs[0]), HD, 1)
    return (top / bottom).astype(jnp.bfloat16)


def lane_masks():
    lane = lax.broadcasted_iota(jnp.int32, (1, LANES), 1)
    low = jnp.where(lane < HD, 1.0, 0.0).astype(jnp.bfloat16)
    high = jnp.where(lane < HD, 0.0, 1.0).astype(jnp.bfloat16)
    return low, high


def block_attention(qkv, att, row, channels, pair, bias, count):
    low, high = lane_masks()
    rows = pl.ds(row, count)
    base = pair * LANES

    def lanes(offset):
        start = base + offset
        return pl.ds(start if isinstance(start, int) else pl.multiple_of(start, LANES), LANES)

    q = qkv[rows, lanes(0)]
    k = qkv[rows, lanes(channels)]
    v = qkv[rows, lanes(2 * channels)]
    att[rows, lanes(0)] = head_pair(q, k, v, bias, low, high)


def split_rows(out_refs, value):
    start = 0
    for out in out_refs:
        out[...] = value[start : start + out.shape[0]].astype(out.dtype)
        start += out.shape[0]


def pack_kernel(plan, keys, maps_hbm, x_hbm, lat_ref, lon_ref, diag_ref, maps_ref, x_ref, sems):
    copies = [
        pltpu.make_async_copy(maps_hbm, maps_ref, sems.at[0]),
        pltpu.make_async_copy(x_hbm, x_ref, sems.at[1]),
    ]
    for copy in copies:
        copy.start()
    copies[0].wait()
    lat_size, diag_size = lat_ref.shape[0], diag_ref.shape[0]
    near = one_hot(maps_ref, keys["near"], lat_size + diag_size)
    far = one_hot(maps_ref, keys["lon"], lon_ref.shape[0])
    copies[1].wait()
    tile = plan.height * plan.width
    strip = HALF_LAT * plan.width
    first_rows = jnp.concatenate([x_ref[lv * tile : lv * tile + strip, :] for lv in range(plan.levels)], 0)
    split_rows((lat_ref, diag_ref), jnp.dot(near, first_rows, preferred_element_type=jnp.float32))
    lon_ref[...] = jnp.dot(far, x_ref[...], preferred_element_type=jnp.float32).astype(lon_ref.dtype)


def fine_first_kernel(
    plan, keys, maps_ref, edge_ref, x_ref, gain_ref, w_ref, wo_ref, y_ref, rest_ref, sent_ref, bias, qkv, att
):
    channels = x_ref.shape[1]
    x = x_ref[...]
    count = plan.window
    tokens = picked(maps_ref, keys["first"], y_ref.shape[0], x)
    normed = normed_rows(tokens, gain_ref[...])
    qkv[...] = jnp.dot(normed, w_ref[...], preferred_element_type=jnp.float32).astype(jnp.bfloat16)
    rest_ref[...] = picked(maps_ref, keys["rest"], rest_ref.shape[0], x).astype(jnp.bfloat16)
    for g in range(plan.groups):
        bias[2 * g] = score_bias(count, plan.group_split[g], 0)
        bias[2 * g + 1] = score_bias(count, plan.group_split[g], edge_ref[0])
    for pair in range(channels // LANES):
        for g in range(plan.groups):
            b = bias[2 * g] if plan.group_split[g] else None
            block_attention(qkv, att, g * count, channels, pair, b, count)
    update = jnp.dot(att[...], wo_ref[...], preferred_element_type=jnp.float32)
    y = (tokens + update).astype(jnp.bfloat16)
    y_ref[...] = y
    sent_ref[...] = picked(maps_ref, keys["sent", "first"], sent_ref.shape[0], y).astype(jnp.bfloat16)


def fine_rest_kernel(
    plan, keys, maps_ref, bias, sent_ref, rest_ref, lat_ref, lon_ref, diag_ref, gain_ref, w_ref, wo_ref,
    y_ref, slat_ref, slon_ref, sdiag_ref, tokens, qkv, att,
):
    channels = rest_ref.shape[1]
    count = plan.window
    block = plan.groups * count
    spread = len(plan.windows) - 1
    raw = {"raw_lat": lat_ref, "raw_lon": lon_ref, "raw_diag": diag_ref}
    for w in range(spread):
        rows = slice(w * block, (w + 1) * block)
        value = rest_ref[rows, :].astype(jnp.float32)
        for name, ref in raw.items():
            if (name, w) in keys:
                value = value + picked(maps_ref, keys[name, w], block, ref[...])
        tokens[rows, :] = value
    normed = normed_rows(tokens[...], gain_ref[...])
    qkv[...] = jnp.dot(normed, w_ref[...], preferred_element_type=jnp.float32).astype(jnp.bfloat16)
    pairs = channels // LANES

    @pl.loop(0, spread)
    def _(w):
        below = jnp.where(w + 1 >= plan.width // WIN_LON, 1, 0)
        for pair in range(pairs):
            for g in range(plan.groups):
                row = pl.multiple_of(w * block + g * count, 16)
                block_attention(qkv, att, row, channels, pair, bias[2 * g + below], count)

    update = jnp.dot(att[...], wo_ref[...], preferred_element_type=jnp.float32)
    y = (tokens[...] + update).astype(jnp.bfloat16)
    y_ref[...] = y
    start = 0
    for name, out in (("res_lat", slat_ref), ("res_lon", slon_ref), ("res_diag", sdiag_ref)):
        size = out.shape[0]
        value = sent_ref[start : start + size, :].astype(jnp.float32)
        for w in range(spread):
            if (name, w) in keys:
                value = value + picked(maps_ref, keys[name, w], size, y[w * block : (w + 1) * block])
        out[...] = value.astype(jnp.bfloat16)
        start += size


def coarse_own_kernel(keys, maps_ref, first_ref, rest_ref, part_ref):
    value = picked(maps_ref, keys["parts", "first"], part_ref.shape[0], first_ref[...])
    value = value + picked(maps_ref, keys["parts", "rest"], part_ref.shape[0], rest_ref[...])
    part_ref[...] = value.astype(jnp.bfloat16)


def thirds(value):
    first = value.astype(jnp.bfloat16).astype(jnp.float32)
    second = (value - first).astype(jnp.bfloat16).astype(jnp.float32)
    return jnp.concatenate([first, second, value - first - second], 0).astype(jnp.bfloat16)


def summed_thirds(stacked, right):
    out = jnp.dot(stacked, right, preferred_element_type=jnp.float32)
    rows = out.shape[0] // 3
    return out[:rows] + out[rows : 2 * rows] + out[2 * rows :]


def coarse_kernel(
    plan, keys, maps_ref, bias, part_ref, lat_ref, lon_ref, diag_ref, gm_ref, wm_ref, gs_ref, ws_ref, wo_ref,
    wsp_ref, weight_ref, fine_ref, upper_ref, sums_ref, qkv, att,
):
    parts = len(plan.parts)
    channels = part_ref.shape[1]
    total = upper_ref.shape[0]
    wide = ws_ref.shape[0]
    count = plan.window
    value = part_ref[...].astype(jnp.float32)
    for name, ref in (("res_lat", lat_ref), ("res_lon", lon_ref), ("res_diag", diag_ref)):
        value = value + picked(maps_ref, keys["parts", name], parts * total, ref[...])
    fine_ref[...] = value.astype(jnp.bfloat16)

    def part(k):
        return fine_ref[k * total : (k + 1) * total, :].astype(jnp.float32)

    mean = sum(jnp.sum(part(k), -1, keepdims=True) for k in range(parts)) / (parts * channels)
    square = sum(jnp.sum((part(k) - mean) ** 2, -1, keepdims=True) for k in range(parts))
    scale = lax.rsqrt(square / (parts * channels) + epsilon)
    merged = 0.0
    for k in range(parts):
        span = slice(k * channels, (k + 1) * channels)
        normed = ((part(k) - mean) * scale * gm_ref[:, span]).astype(jnp.bfloat16)
        merged = merged + jnp.dot(normed, wm_ref[span, :], preferred_element_type=jnp.float32)
    coarse = merged.astype(jnp.bfloat16).astype(jnp.float32)
    normed = normed_rows(coarse, gs_ref[...])
    qkv[...] = jnp.dot(normed, ws_ref[...], preferred_element_type=jnp.float32).astype(jnp.bfloat16)

    at_once = 4

    @pl.loop(0, wide // LANES // at_once)
    def _(step):
        for i in range(at_once):
            for g in range(plan.groups):
                block_attention(qkv, att, g * count, wide, step * at_once + i, bias[2 * g + 1], count)

    update = jnp.dot(att[...], wo_ref[...], preferred_element_type=jnp.float32)
    upper = (coarse + update).astype(jnp.bfloat16)
    upper_ref[...] = upper
    levels = plan.levels
    span = total // levels
    token = lax.broadcasted_iota(jnp.int32, (levels, total), 1)
    level = lax.broadcasted_iota(jnp.int32, (levels, total), 0)
    inside = (token >= level * span) & (token < (level + 1) * span)
    rows = jnp.concatenate([jnp.where(inside, weight_ref[ro : ro + 1, :], 0.0) for ro in range(2)], 0)
    weights = thirds(rows)
    heavy = thirds(summed_thirds(weights, upper))
    spread = summed_thirds(heavy, wsp_ref[...])
    sums = 0.0
    for k in range(parts):
        ro = k // 2
        fine = summed_thirds(weights, fine_ref[k * total : (k + 1) * total, :])
        sums = sums + (fine + spread[:, k * channels : (k + 1) * channels])[ro * levels : (ro + 1) * levels]
    for i, lv in enumerate(plan.order):
        sums_ref[lv : lv + 1, :] = sums[i : i + 1]


def split_kernel(plan, keys, maps_ref, fine_ref, upper_ref, wsp_ref, own_ref, slat_ref, slon_ref, sdiag_ref, decoded):
    parts = len(plan.parts)
    total = upper_ref.shape[0]
    channels = fine_ref.shape[1]
    levels = plan.levels
    span = total // levels
    upper = upper_ref[...]
    for k in range(parts):
        spread = jnp.dot(upper, wsp_ref[:, k * channels : (k + 1) * channels], preferred_element_type=jnp.float32)
        value = (fine_ref[k * total : (k + 1) * total, :].astype(jnp.float32) + spread).astype(jnp.bfloat16)
        for i in range(levels):
            decoded[i, k * span : (k + 1) * span, :] = value[i * span : (i + 1) * span]
    quarter = parts * (span // 4)
    hot = one_hot(maps_ref, keys["quarters"], parts * span)
    for i in range(levels):
        moved = jnp.dot(hot, decoded[i], preferred_element_type=jnp.float32).astype(jnp.bfloat16)
        for q, out in enumerate((own_ref, slon_ref, slat_ref, sdiag_ref)):
            out[i * quarter : (i + 1) * quarter, :] = moved[q * quarter : (q + 1) * quarter]


def output_kernel(plan, keys, maps_ref, own_ref, lon_ref, lat_ref, diag_ref, out_ref):
    span = own_ref.shape[0] // plan.levels
    tile = plan.height * plan.width
    hot = one_hot(maps_ref, keys["output"], tile)
    for i, lv in enumerate(plan.order):
        rows = slice(i * span, (i + 1) * span)
        stacked = jnp.concatenate(
            [ref[rows, :].astype(jnp.float32) for ref in (own_ref, lon_ref, lat_ref, diag_ref)], 0
        ).astype(jnp.bfloat16)
        moved = jnp.dot(hot, stacked, preferred_element_type=jnp.float32)
        out_ref[lv * tile : (lv + 1) * tile, :] = moved.astype(jnp.bfloat16)


def all_summed(value, axes):
    for axis in axes:
        count = lax.axis_size(axis)
        if count & (count - 1):
            value = lax.psum(value, axis)
            continue
        step = 1
        while step < count:
            value = value + lax.ppermute(value, axis, [(i, i ^ step) for i in range(count)])
            step *= 2
    return value


def whole_step(
    latent, gain_first, triple_first, output_first, gain_merge, merge_weight, gain_second, triple_second,
    output_second, split_weight,
):
    levels, height, width, channels = latent.shape
    wide = merge_weight.shape[1]
    plan = Plan(levels, height, width)
    maps = Maps()
    lat_count, lon_count = lax.axis_size("lat"), lax.axis_size("lon")

    def moved(value, lat_step, lon_step):
        pairs = [
            (a * lon_count + b, (a + lat_step) % lat_count * lon_count + (b + lon_step) % lon_count)
            for a in range(lat_count)
            for b in range(lon_count)
        ]
        return lax.ppermute(value, ("lat", "lon"), pairs)

    raw = {"raw_lat": (plan.raw_lat, height, 0), "raw_lon": (plan.raw_lon, 0, width), "raw_diag": (plan.raw_diag, height, width)}
    results = {"res_lat": (plan.res_lat, height, 0), "res_lon": (plan.res_lon, 0, width), "res_diag": (plan.res_diag, height, width)}
    pack_maps = Maps()
    strip = [cell for cell in plan.own if cell[1] < HALF_LAT]
    near = plan.shifted(*raw["raw_lat"]) + plan.shifted(*raw["raw_diag"])
    pack_keys = {
        "near": pack_maps.add(scatter_map(strip, near)),
        "lon": pack_maps.add(scatter_map(plan.own, plan.shifted(*raw["raw_lon"]))),
    }
    keys = {}

    def add(key, source, target):
        vector = scatter_map(source, target)
        if (vector >= 0).any():
            keys[key] = maps.add(vector)

    add("first", plan.own, plan.first)
    add("rest", plan.own, plan.rest)
    add(("sent", "first"), plan.first, sum([plan.shifted(*v) for v in results.values()], []))
    for w, block in enumerate(plan.blocks[1:]):
        for name, (cells, _, _) in raw.items():
            add((name, w), cells, block)
        for name, value in results.items():
            add((name, w), block, plan.shifted(*value))
    all_parts = sum(plan.parts, [])
    add(("parts", "first"), plan.first, all_parts)
    add(("parts", "rest"), plan.rest, all_parts)
    for name, (cells, _, _) in results.items():
        add(("parts", name), cells, all_parts)
    cells = [
        (2 * r + ro, 2 * c + co)
        for ro in range(2)
        for co in range(2)
        for r in range(plan.coarse_rows)
        for c in range(plan.coarse_cols)
    ]
    half_rows, half_cols = height // 2, width // 2
    quarters = [
        (qr * half_rows + r, qc * half_cols + c)
        for qr in range(2)
        for qc in range(2)
        for r in range(half_rows)
        for c in range(half_cols)
    ]
    keys["quarters"] = maps.add(scatter_map(cells, quarters))
    placed = [((r + half_rows) % height, (c + half_cols) % width) for r, c in quarters]
    keys["output"] = maps.add(scatter_map(placed, [(r, c) for r in range(height) for c in range(width)]))
    table, pack_table = maps.array(), pack_maps.array()

    vmem = pl.BlockSpec(memory_space=pltpu.VMEM)
    smem = pl.BlockSpec(memory_space=pltpu.SMEM)
    bf16 = jnp.bfloat16

    def call(body, outs, args, scratch=(), flops=0, limit=16, specs=None):
        size = sum(math.prod(a.shape) * a.dtype.itemsize for a in args)
        return pl.pallas_call(
            body,
            out_shape=[jax.ShapeDtypeStruct(s, d) for s, d in outs],
            in_specs=specs or [smem if a.ndim == 1 else vmem for a in args],
            out_specs=[vmem] * len(outs),
            scratch_shapes=list(scratch),
            cost_estimate=pl.CostEstimate(flops=flops, bytes_accessed=size, transcendentals=0),
            compiler_params=pltpu.CompilerParams(vmem_limit_bytes=limit << 20),
        )(*args)

    def rows_of(*counts):
        return [((n, channels), bf16) for n in counts]

    count = plan.window
    x = latent.reshape(levels * height * width, channels)
    edge = (lax.axis_index("lat") == lat_count - 1).astype(jnp.int32).reshape(1)
    n_first, n_rest, n_coarse = len(plan.first), len(plan.rest), len(plan.parts[0])
    n_part = len(plan.parts)
    n_sent = [len(cells) for cells, _, _ in results.values()]

    hbm = pl.BlockSpec(memory_space=pltpu.HBM)
    s_lat, s_lon, s_diag = call(
        functools.partial(pack_kernel, plan, pack_keys), rows_of(*[len(cells) for cells, _, _ in raw.values()]),
        (pack_table, x),
        [
            pltpu.VMEM(pack_table.shape, jnp.int32),
            pltpu.VMEM(x.shape, bf16),
            pltpu.SemaphoreType.DMA((2,)),
        ],
        flops=10**9, limit=LIMITS["pack"], specs=[hbm, hbm],
    )
    r_lat, r_lon, r_diag = moved(s_lat, -1, 0), moved(s_lon, 0, -1), moved(s_diag, -1, -1)
    gain1 = gain_first.reshape(1, channels)
    y_first, x_rest, sent, bias = call(
        functools.partial(fine_first_kernel, plan, keys),
        rows_of(n_first, n_rest, sum(n_sent)) + [((2 * plan.groups, count, count), jnp.float32)],
        (table, edge, x, gain1, triple_first, output_first),
        [pltpu.VMEM((n_first, 3 * channels), bf16), pltpu.VMEM((n_first, channels), bf16)],
        flops=4 * 10**9, limit=LIMITS["first"],
    )
    y_rest, s_lat, s_lon, s_diag = call(
        functools.partial(fine_rest_kernel, plan, keys), rows_of(n_rest, *n_sent),
        (table, bias, sent, x_rest, r_lat, r_lon, r_diag, gain1, triple_first, output_first),
        [
            pltpu.VMEM((n_rest, channels), jnp.float32),
            pltpu.VMEM((n_rest, 3 * channels), bf16),
            pltpu.VMEM((n_rest, channels), bf16),
        ],
        flops=6 * 10**9, limit=LIMITS["rest"],
    )
    r_lat, r_lon, r_diag = moved(s_lat, -1, 0), moved(s_lon, 0, -1), moved(s_diag, -1, -1)
    (parts,) = call(
        functools.partial(coarse_own_kernel, keys), rows_of(n_part * n_coarse),
        (table, y_first, y_rest), flops=4 * 10**9, limit=LIMITS["own"],
    )
    total_rows = height * lat_count
    total_cols = width * lon_count

    def row_weights(rows):
        return jnp.cos(jnp.pi * ((rows.astype(jnp.float32) + 0.5) / total_rows - 0.5))

    every = row_weights(jnp.arange(total_rows, dtype=jnp.int32))
    scale_total = jnp.sqrt(total_cols * jnp.sum(every * every))
    frame_rows = np.array([[r for _, r, _ in plan.parts[2 * ro]] for ro in range(2)], np.int32)
    weights = row_weights((lax.axis_index("lat") * height + frame_rows) % total_rows) / scale_total
    fine, upper, sums = call(
        functools.partial(coarse_kernel, plan, keys),
        rows_of(n_part * n_coarse) + [((n_coarse, wide), bf16), ((levels, channels), jnp.float32)],
        (
            table, bias, parts, r_lat, r_lon, r_diag, gain_merge.reshape(1, -1), merge_weight,
            gain_second.reshape(1, -1), triple_second, output_second, split_weight, weights,
        ),
        [pltpu.VMEM((n_coarse, 3 * wide), bf16), pltpu.VMEM((n_coarse, wide), bf16)],
        flops=8 * 10**9, limit=LIMITS["coarse"],
    )
    own, s_lat, s_lon, s_diag = call(
        functools.partial(split_kernel, plan, keys), rows_of(*[n_coarse] * 4),
        (table, fine, upper, split_weight), [pltpu.VMEM((levels, n_part * n_coarse // levels, channels), bf16)],
        flops=2 * 10**9, limit=LIMITS["split"],
    )
    d_lat, d_lon, d_diag = (moved(s_lat, 1, 0), moved(s_lon, 0, 1), moved(s_diag, 1, 1))
    means = all_summed(sums, ("lat", "lon"))
    (decoded,) = call(
        functools.partial(output_kernel, plan, keys),
        rows_of(levels * height * width), (table, own, d_lon, d_lat, d_diag), flops=10**9, limit=LIMITS["output"],
    )
    return decoded.reshape(latent.shape), means


def solution(mesh):
    return jax.shard_map(
        whole_step,
        mesh=mesh,
        in_specs=(P(None, "lat", "lon", None), P(), P(), P(), P(), P(), P(), P(), P(), P()),
        out_specs=(P(None, "lat", "lon", None), P()),
        check_vma=False,
    )
```

```python
import functools
import math

import jax
import jax.numpy as jnp
import numpy as np
from jax import lax
from jax.experimental import pallas as pl
from jax.experimental.pallas import tpu as pltpu
from jax.sharding import PartitionSpec as P

HD = 64
WIN_LEV = 2
WIN_LAT = 6
WIN_LON = 12
HALF_LAT = WIN_LAT // 2
HALF_LON = WIN_LON // 2
LANES = 128

epsilon = 1e-05
masked_score = -1e30
score_scale = HD**-0.5 * math.log2(math.e)

LIMITS = {"pack": 59, "first": 16, "edge": 16, "own": 12, "coarse": 16, "split": 8, "output": 8}


class Plan:
    def __init__(self, levels, height, width):
        self.levels, self.height, self.width = levels, height, width
        assert levels % WIN_LEV == 0
        assert height == 2 * WIN_LAT and width == 2 * WIN_LON
        self.groups = levels // WIN_LEV
        half_lev = WIN_LEV // 2
        self.group_levels = [
            [(g * WIN_LEV + half_lev + i) % levels for i in range(WIN_LEV)] for g in range(self.groups)
        ]
        self.order = [lv for group in self.group_levels for lv in group]
        ids = [(((lv + half_lev)) // WIN_LEV) for lv in range(levels)]
        self.group_split = [len({ids[lv] for lv in group}) > 1 for group in self.group_levels]
        self.window = WIN_LEV * WIN_LAT * WIN_LON
        self.windows = [(wr, wc) for wr in range(height // WIN_LAT) for wc in range(width // WIN_LON)]

        self.blocks = [
            cells_of(
                (HALF_LAT + wr * WIN_LAT, HALF_LAT + (wr + 1) * WIN_LAT),
                (HALF_LON + wc * WIN_LON, HALF_LON + (wc + 1) * WIN_LON),
            )
            for wr, wc in self.windows
        ]
        self.own = cells_of((0, height), (0, width))
        fl, fc, fh, fw = HALF_LAT, HALF_LON, height, width
        self.raw = {
            "raw_lat": cells_of((fh, fh + fl), (fc, fw)),
            "raw_diag": cells_of((fh, fh + fl), (fw, fw + fc)),
            "raw_lon": cells_of((fl, fh), (fw, fw + fc)),
        }
        self.results = {
            "res_lat": padded(cells_of((fh + fl, fh + 2 * fl), (2 * fc, fw + fc))),
            "res_lon": padded(cells_of((2 * fl, fh + fl), (fw + fc, fw + 2 * fc))),
            "res_diag": padded(cells_of((fh + fl, fh + 2 * fl), (fw + fc, fw + 2 * fc))),
        }
        self.coarse_rows, self.coarse_cols = height // 2, width // 2
        self.parts = [
            [
                (2 * fl + 2 * r + ro, 2 * fc + 2 * c + co)
                for r in range(self.coarse_rows)
                for c in range(self.coarse_cols)
            ]
            for ro in range(2)
            for co in range(2)
        ]


def cells_of(rows, cols):
    return [(r, c) for r in range(*rows) for c in range(*cols)]


def padded(cells):
    return cells + [None] * (-len(cells) % 8)


def shifted(cells, rows, cols):
    return [cell and (cell[0] - rows, cell[1] - cols) for cell in cells]


def scatter_map(source, target):
    place = {cell: i for i, cell in enumerate(target) if cell is not None}
    return np.array([-1 if cell is None else place.get(cell, -1) for cell in source], np.int32)


class Maps:
    def __init__(self):
        self.rows, self.keys = [], {}

    def add(self, key, source, target):
        self.keys[key] = (len(self.rows), len(source), len(target))
        self.rows.append(scatter_map(source, target))

    def array(self):
        width = -(-max(len(v) for v in self.rows) // LANES) * LANES
        height = -(-len(self.rows) // 8) * 8
        out = np.full((height, width), -1, np.int32)
        for i, v in enumerate(self.rows):
            out[i, : len(v)] = v
        return jnp.asarray(out)


def table_hot(maps_ref, key):
    row, count, out_rows = key
    return one_hot(maps_ref[row : row + 1, :count], out_rows)


def one_hot(index, out_rows):
    hot = lax.broadcasted_iota(jnp.int32, (out_rows, index.shape[1]), 0) == index
    return jnp.where(hot, 1.0, 0.0).astype(jnp.bfloat16)


def box_hot(levels, rows, cols, boxes, out_rows, turn=0):
    token = lax.broadcasted_iota(jnp.int32, (1, levels * rows * cols), 1)

    def divided(value, by):
        return jnp.floor((value.astype(jnp.float32) + 0.5) * (1.0 / by)).astype(jnp.int32)

    level = divided(token, rows * cols)
    inner = token - level * (rows * cols)
    row = divided(inner, cols)
    col = inner - row * cols
    slot = jnp.where(level >= turn, level - turn, level + levels - turn)
    place = jnp.full_like(token, -1)
    for r0, r1, c0, c1, base, level_step, row_step in boxes:
        inside = (row >= r0) & (row < r1) & (col >= c0) & (col < c1)
        place = jnp.where(inside, base + slot * level_step + (row - r0) * row_step + (col - c0), place)
    return one_hot(place, out_rows)


def moved_rows(hot, source):
    return jnp.dot(hot, source, preferred_element_type=jnp.float32)


def normed_rows(value, gain):
    mean = jnp.mean(value, -1, keepdims=True)
    centred = value - mean
    var = jnp.mean(centred * centred, -1, keepdims=True)
    return (centred * lax.rsqrt(var + epsilon) * gain).astype(jnp.bfloat16)


def score_bias(count, group_split, edge):
    span = count // WIN_LEV
    rows = lax.broadcasted_iota(jnp.int32, (count, count), 0)
    cols = lax.broadcasted_iota(jnp.int32, (count, count), 1)
    q_lev, k_lev = rows >= span, cols >= span
    q_in = rows - jnp.where(q_lev, span, 0)
    k_in = cols - jnp.where(k_lev, span, 0)
    half = span // 2
    apart = (q_in >= half) != (k_in >= half)
    apart = jnp.where(apart, edge, 0)
    if group_split:
        apart = jnp.where(q_lev != k_lev, 1, apart)
    return jnp.where(apart > 0, masked_score, 0.0)


def head_pair(q, k, v, bias, low, high):
    trans = (((1,), (1,)), ((), ()))
    outs = []
    for keep, fill in ((low, high), (high, low)):
        s = lax.dot_general(q, k * keep, trans, preferred_element_type=jnp.float32)
        if bias is not None:
            s = s + bias
        peak = jnp.max(s, -1, keepdims=True)
        p = jnp.exp2((s - peak) * score_scale).astype(jnp.bfloat16)
        outs.append(jnp.dot(p, v * keep + fill, preferred_element_type=jnp.float32))
    is_low = lax.broadcasted_iota(jnp.int32, outs[0].shape, 1) < HD
    top = jnp.where(is_low, outs[0], outs[1])
    bottom = pltpu.roll(jnp.where(is_low, outs[1], outs[0]), HD, 1)
    return (top / bottom).astype(jnp.bfloat16)


def lane_masks():
    lane = lax.broadcasted_iota(jnp.int32, (1, LANES), 1)
    low = jnp.where(lane < HD, 1.0, 0.0).astype(jnp.bfloat16)
    high = jnp.where(lane < HD, 0.0, 1.0).astype(jnp.bfloat16)
    return low, high


def block_attention(qkv, att, row, channels, pair, bias, count):
    low, high = lane_masks()
    rows = pl.ds(row, count)
    base = pair * LANES

    def lanes(offset):
        start = base + offset
        return pl.ds(start if isinstance(start, int) else pl.multiple_of(start, LANES), LANES)

    q = qkv[rows, lanes(0)]
    k = qkv[rows, lanes(channels)]
    v = qkv[rows, lanes(2 * channels)]
    att[rows, lanes(0)] = head_pair(q, k, v, bias, low, high)


def split_rows(out_refs, value):
    start = 0
    for out in out_refs:
        out[...] = value[start : start + out.shape[0]].astype(out.dtype)
        start += out.shape[0]


def pack_kernel(plan, x_hbm, lat_ref, diag_ref, lon_ref, near_ref, far_ref, sems):
    levels, height, width = plan.levels, plan.height, plan.width
    fl, fc = HALF_LAT, HALF_LON
    copies = [
        pltpu.make_async_copy(x_hbm.at[:, 0:fl], near_ref, sems.at[0]),
        pltpu.make_async_copy(x_hbm.at[:, fl:height, 0 : far_ref.shape[2]], far_ref, sems.at[1]),
    ]
    for copy in copies:
        copy.start()
    turn = WIN_LEV // 2
    across, down = width - fc, height - fl
    lat_size, diag_size = lat_ref.shape[0], diag_ref.shape[0]
    near = box_hot(
        levels, fl, width,
        [(0, fl, fc, width, 0, fl * across, across), (0, fl, 0, fc, lat_size, fl * fc, fc)],
        lat_size + diag_size, turn,
    )
    far = box_hot(levels, down, far_ref.shape[2], [(0, down, 0, fc, 0, down * fc, fc)], lon_ref.shape[0], turn)
    channels = x_hbm.shape[-1]
    copies[0].wait()
    split_rows((lat_ref, diag_ref), moved_rows(near, near_ref[...].reshape(-1, channels)))
    copies[1].wait()
    lon_ref[...] = moved_rows(far, far_ref[...].reshape(-1, channels)).astype(lon_ref.dtype)


def fine_first_kernel(
    plan, edge_ref, x_ref, gain_ref, w_ref, wo_ref, y_ref, *more
):
    rest_refs, (slat_ref, slon_ref, sdiag_ref, bias, qkv, att) = more[:-6], more[-6:]
    channels = x_ref.shape[1]
    levels, height, width = plan.levels, plan.height, plan.width
    fl, fc = HALF_LAT, HALF_LON
    turn = WIN_LEV // 2
    x = x_ref[...]
    count = plan.window
    area = WIN_LAT * WIN_LON
    block = y_ref.shape[0]

    def window_box(w, base):
        wr, wc = plan.windows[w]
        r0, c0 = fl + wr * WIN_LAT, fc + wc * WIN_LON
        return (r0, min(r0 + WIN_LAT, height), c0, min(c0 + WIN_LON, width), base, area, WIN_LON)

    tokens = moved_rows(box_hot(levels, height, width, [window_box(0, 0)], block, turn), x)
    normed = normed_rows(tokens, gain_ref[...])
    qkv[...] = jnp.dot(normed, w_ref[...], preferred_element_type=jnp.float32).astype(jnp.bfloat16)
    for w in range(1, len(plan.windows)):
        hot = box_hot(levels, height, width, [window_box(w, 0)], block, turn)
        rest_refs[w - 1][...] = moved_rows(hot, x).astype(jnp.bfloat16)
    for g in range(plan.groups):
        bias[2 * g] = score_bias(count, plan.group_split[g], 0)
        bias[2 * g + 1] = score_bias(count, plan.group_split[g], edge_ref[0])
    for pair in range(channels // LANES):
        for g in range(plan.groups):
            b = bias[2 * g] if plan.group_split[g] else None
            block_attention(qkv, att, g * count, channels, pair, b, count)
    update = jnp.dot(att[...], wo_ref[...], preferred_element_type=jnp.float32)
    y = (tokens + update).astype(jnp.bfloat16)
    y_ref[...] = y
    split_rows((slat_ref, slon_ref, sdiag_ref), moved_rows(sent_hot(plan, 0, sum(sent_sizes(plan))), y))


def sent_sizes(plan):
    return [plan.levels * len(cells) for cells in plan.results.values()]


def sent_hot(plan, w, out_rows, only=None):
    boxes, start = [], 0
    shifts = {"res_lat": (plan.height, 0), "res_lon": (0, plan.width), "res_diag": (plan.height, plan.width)}
    for name, cells in plan.results.items():
        sent = [cell for cell in shifted(cells, *shifts[name]) if cell is not None]
        r0, c0 = sent[0]
        r1, c1 = sent[-1]
        w0, v0 = plan.blocks[w][0]
        top, left = max(r0, w0), max(c0, v0)
        bottom, right = min(r1 + 1, w0 + WIN_LAT), min(c1 + 1, v0 + WIN_LON)
        if top < bottom and left < right and only in (None, name):
            row_step = c1 + 1 - c0
            base = start + (top - r0) * row_step + (left - c0)
            boxes.append((top - w0, bottom - w0, left - v0, right - v0, base, len(cells), row_step))
        if only is None:
            start += plan.levels * len(cells)
    if not boxes:
        return None
    return box_hot(plan.levels, WIN_LAT, WIN_LON, boxes, out_rows)


def raw_hot(plan, name, w, out_rows):
    cells = plan.raw[name]
    (r0, c0), (r1, c1) = cells[0], cells[-1]
    w0, v0 = plan.blocks[w][0]
    top, left = max(r0, w0), max(c0, v0)
    bottom, right = min(r1 + 1, w0 + WIN_LAT), min(c1 + 1, v0 + WIN_LON)
    if not (top < bottom and left < right):
        return None
    base = (top - w0) * WIN_LON + (left - v0)
    box = (top - r0, bottom - r0, left - c0, right - c0, base, WIN_LAT * WIN_LON, WIN_LON)
    return box_hot(plan.levels, r1 + 1 - r0, c1 + 1 - c0, [box], out_rows)


def fine_windows(plan, which, bias, rest_ref, raw, gain_ref, w_ref, wo_ref, y_ref, tokens, qkv, att):
    channels = rest_ref.shape[1]
    count = plan.window
    block = plan.groups * count
    for i, w in enumerate(which):
        value = rest_ref[i * block : (i + 1) * block, :].astype(jnp.float32)
        for name, ref in raw.items():
            hot = raw_hot(plan, name, w, block)
            if hot is not None:
                value = value + moved_rows(hot, ref[...])
        tokens[i * block : (i + 1) * block, :] = value
    normed = normed_rows(tokens[...], gain_ref[...])
    qkv[...] = jnp.dot(normed, w_ref[...], preferred_element_type=jnp.float32).astype(jnp.bfloat16)

    def window(i, below):
        for pair in range(channels // LANES):
            for g in range(plan.groups):
                row = i * block + g * count
                if not isinstance(row, int):
                    row = pl.multiple_of(row, 16)
                block_attention(qkv, att, row, channels, pair, bias[2 * g + below], count)

    belows = [plan.windows[w][0] for w in which]
    if len(which) == 1:
        window(0, belows[0])
    else:
        assert belows == list(range(len(which)))

        @pl.loop(0, len(which))
        def _(i):
            window(i, i)

    update = jnp.dot(att[...], wo_ref[...], preferred_element_type=jnp.float32)
    y = (tokens[...] + update).astype(jnp.bfloat16)
    y_ref[...] = y
    return y


def fine_edge_kernel(plan, w, name, raw_names, bias, sent_ref, rest_ref, *more):
    raw = dict(zip(raw_names, more))
    gain_ref, w_ref, wo_ref, y_ref, out_ref, tokens, qkv, att = more[len(raw_names) :]
    y = fine_windows(plan, [w], bias, rest_ref, raw, gain_ref, w_ref, wo_ref, y_ref, tokens, qkv, att)
    moved = moved_rows(sent_hot(plan, w, out_ref.shape[0], name), y)
    out_ref[...] = (sent_ref[...].astype(jnp.float32) + moved).astype(jnp.bfloat16)


def coarse_own_kernel(
    plan, keys, which, maps_ref, bias, first_ref, right_ref, below_ref, rest_ref, lat_ref, diag_ref, lon_ref, gain_ref, w_ref,
    wo_ref, part_ref, y_ref, tokens, qkv, att,
):
    raw = {"raw_lat": lat_ref, "raw_diag": diag_ref, "raw_lon": lon_ref}
    fine_windows(plan, which, bias, rest_ref, raw, gain_ref, w_ref, wo_ref, y_ref, tokens, qkv, att)
    area = WIN_LAT * WIN_LON
    hot = table_hot(maps_ref, keys["own"])
    total = part_ref.shape[0] // len(plan.parts)
    for i in range(plan.levels):
        rows = slice(i * area, (i + 1) * area)
        stacked = jnp.concatenate([ref[rows, :] for ref in (first_ref, right_ref, below_ref, y_ref)], 0)
        value = moved_rows(hot, stacked).astype(jnp.bfloat16)
        for k in range(len(plan.parts)):
            start = k * total + i * area
            part_ref[start : start + area, :] = value[k * area : (k + 1) * area]


def thirds(value):
    first = value.astype(jnp.bfloat16).astype(jnp.float32)
    second = (value - first).astype(jnp.bfloat16).astype(jnp.float32)
    return jnp.concatenate([first, second, value - first - second], 0).astype(jnp.bfloat16)


def summed_thirds(stacked, right):
    out = jnp.dot(stacked, right, preferred_element_type=jnp.float32)
    rows = out.shape[0] // 3
    return out[:rows] + out[rows : 2 * rows] + out[2 * rows :]


def coarse_kernel(
    plan, keys, maps_ref, bias, part_ref, lat_ref, lon_ref, diag_ref, gm_ref, wm_ref, gs_ref, ws_ref, wo_ref,
    wsp_ref, lat_index_ref, weight_ref, fine_ref, upper_ref, sums_ref, qkv, att,
):
    parts = len(plan.parts)
    channels = part_ref.shape[1]
    total = upper_ref.shape[0]
    wide = ws_ref.shape[0]
    count = plan.window
    levels = plan.levels
    area = total // levels
    hot = table_hot(maps_ref, keys["ahead"])
    for i in range(levels):
        pieces = []
        for ref in (lat_ref, lon_ref, diag_ref):
            size = ref.shape[0] // levels
            pieces.append(ref[i * size : (i + 1) * size, :])
        value = moved_rows(hot, jnp.concatenate(pieces, 0))
        for k in range(parts):
            rows = slice(k * total + i * area, k * total + (i + 1) * area)
            own = part_ref[rows, :].astype(jnp.float32)
            fine_ref[rows, :] = (own + value[k * area : (k + 1) * area]).astype(jnp.bfloat16)

    def part(k):
        return fine_ref[k * total : (k + 1) * total, :].astype(jnp.float32)

    mean = sum(jnp.sum(part(k), -1, keepdims=True) for k in range(parts)) / (parts * channels)
    square = sum(jnp.sum((part(k) - mean) ** 2, -1, keepdims=True) for k in range(parts))
    scale = lax.rsqrt(square / (parts * channels) + epsilon)
    merged = 0.0
    for k in range(parts):
        span = slice(k * channels, (k + 1) * channels)
        normed = ((part(k) - mean) * scale * gm_ref[:, span]).astype(jnp.bfloat16)
        merged = merged + jnp.dot(normed, wm_ref[span, :], preferred_element_type=jnp.float32)
    coarse = merged.astype(jnp.bfloat16).astype(jnp.float32)
    normed = normed_rows(coarse, gs_ref[...])
    qkv[...] = jnp.dot(normed, ws_ref[...], preferred_element_type=jnp.float32).astype(jnp.bfloat16)

    at_once = 4

    @pl.loop(0, wide // LANES // at_once)
    def _(step):
        for i in range(at_once):
            for g in range(plan.groups):
                block_attention(qkv, att, g * count, wide, step * at_once + i, bias[2 * g + 1], count)

    update = jnp.dot(att[...], wo_ref[...], preferred_element_type=jnp.float32)
    upper = (coarse + update).astype(jnp.bfloat16)
    upper_ref[...] = upper
    span = total // levels
    token = lax.broadcasted_iota(jnp.int32, (levels, total), 1)
    level = lax.broadcasted_iota(jnp.int32, (levels, total), 0)
    inside = (token >= level * span) & (token < (level + 1) * span)
    mine = weight_ref[lat_index_ref[0]]
    rows = jnp.concatenate([jnp.where(inside, mine[ro : ro + 1, :], 0.0) for ro in range(2)], 0)
    weights = thirds(rows)
    heavy = thirds(summed_thirds(weights, upper))
    spread = summed_thirds(heavy, wsp_ref[...])
    sums = 0.0
    for k in range(parts):
        ro = k // 2
        fine = summed_thirds(weights, fine_ref[k * total : (k + 1) * total, :])
        sums = sums + (fine + spread[:, k * channels : (k + 1) * channels])[ro * levels : (ro + 1) * levels]
    for i, lv in enumerate(plan.order):
        sums_ref[lv : lv + 1, :] = sums[i : i + 1]


def split_kernel(plan, keys, maps_ref, fine_ref, upper_ref, wsp_ref, own_ref, slat_ref, slon_ref, sdiag_ref, decoded):
    parts = len(plan.parts)
    total = upper_ref.shape[0]
    channels = fine_ref.shape[1]
    levels = plan.levels
    span = total // levels
    upper = upper_ref[...]
    for k in range(parts):
        spread = jnp.dot(upper, wsp_ref[:, k * channels : (k + 1) * channels], preferred_element_type=jnp.float32)
        value = (fine_ref[k * total : (k + 1) * total, :].astype(jnp.float32) + spread).astype(jnp.bfloat16)
        for i in range(levels):
            decoded[i, k * span : (k + 1) * span, :] = value[i * span : (i + 1) * span]
    quarter = parts * (span // 4)
    hot = table_hot(maps_ref, keys["quarters"])
    for i in range(levels):
        moved = jnp.dot(hot, decoded[i], preferred_element_type=jnp.float32).astype(jnp.bfloat16)
        for q, out in enumerate((own_ref, slon_ref, slat_ref, sdiag_ref)):
            out[i * quarter : (i + 1) * quarter, :] = moved[q * quarter : (q + 1) * quarter]


def output_kernel(plan, keys, maps_ref, own_ref, lon_ref, lat_ref, diag_ref, out_ref):
    span = own_ref.shape[0] // plan.levels
    tile = plan.height * plan.width
    hot = table_hot(maps_ref, keys["output"])
    for i, lv in enumerate(plan.order):
        rows = slice(i * span, (i + 1) * span)
        stacked = jnp.concatenate(
            [ref[rows, :].astype(jnp.float32) for ref in (own_ref, lon_ref, lat_ref, diag_ref)], 0
        ).astype(jnp.bfloat16)
        moved = jnp.dot(hot, stacked, preferred_element_type=jnp.float32)
        out_ref[lv * tile : (lv + 1) * tile, :] = moved.astype(jnp.bfloat16)


def all_summed(value, axes):
    for axis in axes:
        count = lax.axis_size(axis)
        if count & (count - 1):
            value = lax.psum(value, axis)
            continue
        step = 1
        while step < count:
            value = value + lax.ppermute(value, axis, [(i, i ^ step) for i in range(count)])
            step *= 2
    return value


def whole_step(
    latent, gain_first, triple_first, output_first, gain_merge, merge_weight, gain_second, triple_second,
    output_second, split_weight,
):
    levels, height, width, channels = latent.shape
    wide = merge_weight.shape[1]
    plan = Plan(levels, height, width)
    maps = Maps()
    lat_count, lon_count = lax.axis_size("lat"), lax.axis_size("lon")

    def moved(value, lat_step, lon_step):
        pairs = [
            (a * lon_count + b, (a + lat_step) % lat_count * lon_count + (b + lon_step) % lon_count)
            for a in range(lat_count)
            for b in range(lon_count)
        ]
        return lax.ppermute(value, ("lat", "lon"), pairs)

    all_parts = sum(plan.parts, [])
    maps.add("own", sum(plan.blocks, []), all_parts)
    maps.add("ahead", sum(plan.results.values(), []), all_parts)
    cells = [
        (2 * r + ro, 2 * c + co)
        for ro in range(2)
        for co in range(2)
        for r in range(plan.coarse_rows)
        for c in range(plan.coarse_cols)
    ]
    half_rows, half_cols = height // 2, width // 2
    quarters = [
        (qr * half_rows + r, qc * half_cols + c)
        for qr in range(2)
        for qc in range(2)
        for r in range(half_rows)
        for c in range(half_cols)
    ]
    maps.add("quarters", cells, quarters)
    placed = [((r + half_rows) % height, (c + half_cols) % width) for r, c in quarters]
    maps.add("output", placed, plan.own)
    table, keys = maps.array(), maps.keys

    vmem = pl.BlockSpec(memory_space=pltpu.VMEM)
    smem = pl.BlockSpec(memory_space=pltpu.SMEM)
    bf16 = jnp.bfloat16

    def call(body, outs, args, scratch=(), flops=0, limit=16, specs=None):
        size = sum(math.prod(a.shape) * a.dtype.itemsize for a in args)
        return pl.pallas_call(
            body,
            out_shape=[jax.ShapeDtypeStruct(s, d) for s, d in outs],
            in_specs=specs or [smem if a.ndim == 1 else vmem for a in args],
            out_specs=[vmem] * len(outs),
            scratch_shapes=list(scratch),
            cost_estimate=pl.CostEstimate(flops=flops, bytes_accessed=size, transcendentals=0),
            compiler_params=pltpu.CompilerParams(vmem_limit_bytes=limit << 20),
        )(*args)

    def rows_of(*counts):
        return [((n, channels), bf16) for n in counts]

    count = plan.window
    x = latent.reshape(levels * height * width, channels)
    lat_index = lax.axis_index("lat").astype(jnp.int32)
    edge = (lat_index == lat_count - 1).astype(jnp.int32).reshape(1)
    n_block = plan.groups * count
    n_coarse = levels * len(plan.parts[0])
    n_part = len(plan.parts)
    n_sent = sent_sizes(plan)

    hbm = pl.BlockSpec(memory_space=pltpu.HBM)
    margin = -(-HALF_LON // 8) * 8
    s_lat, s_diag, s_lon = call(
        functools.partial(pack_kernel, plan),
        rows_of(*[levels * len(cells) for cells in plan.raw.values()]), (latent,),
        [
            pltpu.VMEM((levels, HALF_LAT, width, channels), bf16),
            pltpu.VMEM((levels, height - HALF_LAT, margin, channels), bf16),
            pltpu.SemaphoreType.DMA((2,)),
        ],
        flops=10**9, limit=LIMITS["pack"], specs=[hbm],
    )
    r_lat = moved(s_lat, -1, 0)
    r_diag = moved(s_diag, -1, -1)
    r_lon = moved(s_lon, 0, -1)
    gain1 = gain_first.reshape(1, channels)
    y_first, x_right, x_below, x_last, s_lat, s_lon, s_diag, bias = call(
        functools.partial(fine_first_kernel, plan),
        rows_of(n_block, *[n_block] * (len(plan.windows) - 1), *n_sent)
        + [((2 * plan.groups, count, count), jnp.float32)],
        (edge, x, gain1, triple_first, output_first),
        [pltpu.VMEM((n_block, 3 * channels), bf16), pltpu.VMEM((n_block, channels), bf16)],
        flops=4 * 10**9, limit=LIMITS["first"],
    )
    fine_scratch = [
        pltpu.VMEM((n_block, channels), jnp.float32),
        pltpu.VMEM((n_block, 3 * channels), bf16),
        pltpu.VMEM((n_block, channels), bf16),
    ]
    fine_weights = (gain1, triple_first, output_first)

    def fine_edge(w, direction, sent, rest, raws):
        return call(
            functools.partial(fine_edge_kernel, plan, w, direction, list(raws)),
            rows_of(n_block, sent.shape[0]), (bias, sent, rest, *raws.values(), *fine_weights),
            fine_scratch, flops=2 * 10**9, limit=LIMITS["edge"],
        )

    y_right, s_lat = fine_edge(1, "res_lat", s_lat, x_right, {"raw_lon": r_lon})
    q_lat = moved(s_lat, -1, 0)
    q_diag = moved(s_diag, -1, -1)
    y_below, s_lon = fine_edge(2, "res_lon", s_lon, x_below, {"raw_lat": r_lat})
    q_lon = moved(s_lon, 0, -1)
    (parts,) = call(
        functools.partial(coarse_own_kernel, plan, keys, [len(plan.windows) - 1]),
        rows_of(n_part * n_coarse),
        (table, bias, y_first, y_right, y_below, x_last, r_lat, r_diag, r_lon, *fine_weights),
        [pltpu.VMEM((n_block, channels), bf16)] + fine_scratch, flops=4 * 10**9, limit=LIMITS["own"],
    )
    total_rows, total_cols = height * lat_count, width * lon_count
    angle = np.pi * ((np.arange(total_rows) + 0.5) / total_rows - 0.5)
    every = np.cos(angle)
    scaled = every / np.sqrt(total_cols * np.sum(every * every))
    frame_rows = np.array([[r for r, _ in plan.parts[2 * ro]] * levels for ro in range(2)])
    row_of = (np.arange(lat_count)[:, None, None] * height + frame_rows) % total_rows
    weights = jnp.asarray(scaled[row_of], jnp.float32)
    fine, upper, sums = call(
        functools.partial(coarse_kernel, plan, keys),
        rows_of(n_part * n_coarse) + [((n_coarse, wide), bf16), ((levels, channels), jnp.float32)],
        (
            table, bias, parts, q_lat, q_lon, q_diag, gain_merge.reshape(1, -1), merge_weight,
            gain_second.reshape(1, -1), triple_second, output_second, split_weight, lat_index.reshape(1), weights,
        ),
        [pltpu.VMEM((n_coarse, 3 * wide), bf16), pltpu.VMEM((n_coarse, wide), bf16)],
        flops=8 * 10**9, limit=LIMITS["coarse"],
    )
    own, s_lat, s_lon, s_diag = call(
        functools.partial(split_kernel, plan, keys), rows_of(*[n_coarse] * 4),
        (table, fine, upper, split_weight), [pltpu.VMEM((levels, n_part * n_coarse // levels, channels), bf16)],
        flops=2 * 10**9, limit=LIMITS["split"],
    )
    d_lat, d_lon, d_diag = (moved(s_lat, 1, 0), moved(s_lon, 0, 1), moved(s_diag, 1, 1))
    means = all_summed(sums, ("lat", "lon"))
    (decoded,) = call(
        functools.partial(output_kernel, plan, keys),
        rows_of(levels * height * width), (table, own, d_lon, d_lat, d_diag), flops=10**9, limit=LIMITS["output"],
    )
    return decoded.reshape(latent.shape), means


def solution(mesh):
    return jax.shard_map(
        whole_step,
        mesh=mesh,
        in_specs=(P(None, "lat", "lon", None), P(), P(), P(), P(), P(), P(), P(), P(), P()),
        out_specs=(P(None, "lat", "lon", None), P()),
        check_vma=False,
    )
```

```python
import functools
import math

import jax
import jax.numpy as jnp
import numpy as np
from jax import lax
from jax.experimental import pallas as pl
from jax.experimental.pallas import tpu as pltpu
from jax.sharding import PartitionSpec as P

HD = 64
WIN_LEV = 2
WIN_LAT = 6
WIN_LON = 12
HALF_LAT = WIN_LAT // 2
HALF_LON = WIN_LON // 2
LANES = 128

epsilon = 1e-05
masked_score = -1e30
score_scale = HD**-0.5 * math.log2(math.e)

LIMITS = {"pack": 59, "first": 16, "edge": 16, "own": 12, "coarse": 16, "split": 8, "output": 8}


class Plan:
    def __init__(self, levels, height, width):
        self.levels, self.height, self.width = levels, height, width
        assert levels % WIN_LEV == 0
        assert height == 2 * WIN_LAT and width == 2 * WIN_LON
        self.groups = levels // WIN_LEV
        half_lev = WIN_LEV // 2
        self.group_levels = [
            [(g * WIN_LEV + half_lev + i) % levels for i in range(WIN_LEV)] for g in range(self.groups)
        ]
        self.order = [lv for group in self.group_levels for lv in group]
        ids = [(((lv + half_lev)) // WIN_LEV) for lv in range(levels)]
        self.group_split = [len({ids[lv] for lv in group}) > 1 for group in self.group_levels]
        self.window = WIN_LEV * WIN_LAT * WIN_LON
        self.windows = [(wr, wc) for wr in range(height // WIN_LAT) for wc in range(width // WIN_LON)]

        self.blocks = [
            cells_of(
                (HALF_LAT + wr * WIN_LAT, HALF_LAT + (wr + 1) * WIN_LAT),
                (HALF_LON + wc * WIN_LON, HALF_LON + (wc + 1) * WIN_LON),
            )
            for wr, wc in self.windows
        ]
        self.own = cells_of((0, height), (0, width))
        fl, fc, fh, fw = HALF_LAT, HALF_LON, height, width
        self.raw = {
            "raw_lat": cells_of((fh, fh + fl), (fc, fw)),
            "raw_diag": cells_of((fh, fh + fl), (fw, fw + fc)),
            "raw_lon": cells_of((fl, fh), (fw, fw + fc)),
        }
        self.results = {
            "res_lat": padded(cells_of((fh + fl, fh + 2 * fl), (2 * fc, fw + fc))),
            "res_lon": padded(cells_of((2 * fl, fh + fl), (fw + fc, fw + 2 * fc))),
            "res_diag": padded(cells_of((fh + fl, fh + 2 * fl), (fw + fc, fw + 2 * fc))),
        }
        self.coarse_rows, self.coarse_cols = height // 2, width // 2
        self.parts = [
            [
                (2 * fl + 2 * r + ro, 2 * fc + 2 * c + co)
                for r in range(self.coarse_rows)
                for c in range(self.coarse_cols)
            ]
            for ro in range(2)
            for co in range(2)
        ]


def cells_of(rows, cols):
    return [(r, c) for r in range(*rows) for c in range(*cols)]


def padded(cells):
    return cells + [None] * (-len(cells) % 8)


def shifted(cells, rows, cols):
    return [cell and (cell[0] - rows, cell[1] - cols) for cell in cells]


def scatter_map(source, target):
    place = {cell: i for i, cell in enumerate(target) if cell is not None}
    return np.array([-1 if cell is None else place.get(cell, -1) for cell in source], np.int32)


class Maps:
    def __init__(self):
        self.rows, self.keys = [], {}

    def add(self, key, source, target):
        self.keys[key] = (len(self.rows), len(source), len(target))
        self.rows.append(scatter_map(source, target))

    def array(self):
        width = -(-max(len(v) for v in self.rows) // LANES) * LANES
        height = -(-len(self.rows) // 8) * 8
        out = np.full((height, width), -1, np.int32)
        for i, v in enumerate(self.rows):
            out[i, : len(v)] = v
        return jnp.asarray(out)


def table_hot(maps_ref, key):
    row, count, out_rows = key
    return one_hot(maps_ref[row : row + 1, :count], out_rows)


def one_hot(index, out_rows):
    hot = lax.broadcasted_iota(jnp.int32, (out_rows, index.shape[1]), 0) == index
    return jnp.where(hot, 1.0, 0.0).astype(jnp.bfloat16)


def box_hot(levels, rows, cols, boxes, out_rows, turn=0):
    token = lax.broadcasted_iota(jnp.int32, (1, levels * rows * cols), 1)

    def divided(value, by):
        return jnp.floor((value.astype(jnp.float32) + 0.5) * (1.0 / by)).astype(jnp.int32)

    level = divided(token, rows * cols)
    inner = token - level * (rows * cols)
    row = divided(inner, cols)
    col = inner - row * cols
    slot = jnp.where(level >= turn, level - turn, level + levels - turn)
    place = jnp.full_like(token, -1)
    for r0, r1, c0, c1, base, level_step, row_step in boxes:
        inside = (row >= r0) & (row < r1) & (col >= c0) & (col < c1)
        place = jnp.where(inside, base + slot * level_step + (row - r0) * row_step + (col - c0), place)
    return one_hot(place, out_rows)


def moved_rows(hot, source):
    return jnp.dot(hot, source, preferred_element_type=jnp.float32)


def normed_rows(value, gain):
    mean = jnp.mean(value, -1, keepdims=True)
    centred = value - mean
    var = jnp.mean(centred * centred, -1, keepdims=True)
    return (centred * lax.rsqrt(var + epsilon) * gain).astype(jnp.bfloat16)


def score_bias(count, group_split, edge):
    span = count // WIN_LEV
    rows = lax.broadcasted_iota(jnp.int32, (count, count), 0)
    cols = lax.broadcasted_iota(jnp.int32, (count, count), 1)
    q_lev, k_lev = rows >= span, cols >= span
    q_in = rows - jnp.where(q_lev, span, 0)
    k_in = cols - jnp.where(k_lev, span, 0)
    half = span // 2
    apart = (q_in >= half) != (k_in >= half)
    apart = jnp.where(apart, edge, 0)
    if group_split:
        apart = jnp.where(q_lev != k_lev, 1, apart)
    return jnp.where(apart > 0, masked_score, 0.0)


def head_pair(q, k, v, bias, low, high):
    trans = (((1,), (1,)), ((), ()))
    outs = []
    for keep, fill in ((low, high), (high, low)):
        s = lax.dot_general(q, k * keep, trans, preferred_element_type=jnp.float32)
        if bias is not None:
            s = s + bias
        peak = jnp.max(s, -1, keepdims=True)
        p = jnp.exp2((s - peak) * score_scale).astype(jnp.bfloat16)
        outs.append(jnp.dot(p, v * keep + fill, preferred_element_type=jnp.float32))
    is_low = lax.broadcasted_iota(jnp.int32, outs[0].shape, 1) < HD
    top = jnp.where(is_low, outs[0], outs[1])
    bottom = pltpu.roll(jnp.where(is_low, outs[1], outs[0]), HD, 1)
    return (top / bottom).astype(jnp.bfloat16)


def lane_masks():
    lane = lax.broadcasted_iota(jnp.int32, (1, LANES), 1)
    low = jnp.where(lane < HD, 1.0, 0.0).astype(jnp.bfloat16)
    high = jnp.where(lane < HD, 0.0, 1.0).astype(jnp.bfloat16)
    return low, high


def block_attention(qkv, att, row, channels, pair, bias, count):
    low, high = lane_masks()
    rows = pl.ds(row, count)
    base = pair * LANES

    def lanes(offset):
        start = base + offset
        return pl.ds(start if isinstance(start, int) else pl.multiple_of(start, LANES), LANES)

    q = qkv[rows, lanes(0)]
    k = qkv[rows, lanes(channels)]
    v = qkv[rows, lanes(2 * channels)]
    att[rows, lanes(0)] = head_pair(q, k, v, bias, low, high)


def split_rows(out_refs, value):
    start = 0
    for out in out_refs:
        out[...] = value[start : start + out.shape[0]].astype(out.dtype)
        start += out.shape[0]


def pack_kernel(plan, x_hbm, lat_ref, diag_ref, lon_ref, near_ref, far_ref, sems):
    levels, height, width = plan.levels, plan.height, plan.width
    fl, fc = HALF_LAT, HALF_LON
    copies = [
        pltpu.make_async_copy(x_hbm.at[:, 0:fl], near_ref, sems.at[0]),
        pltpu.make_async_copy(x_hbm.at[:, fl:height, 0 : far_ref.shape[2]], far_ref, sems.at[1]),
    ]
    for copy in copies:
        copy.start()
    turn = WIN_LEV // 2
    across, down = width - fc, height - fl
    lat_size, diag_size = lat_ref.shape[0], diag_ref.shape[0]
    near = box_hot(
        levels, fl, width,
        [(0, fl, fc, width, 0, fl * across, across), (0, fl, 0, fc, lat_size, fl * fc, fc)],
        lat_size + diag_size, turn,
    )
    far = box_hot(levels, down, far_ref.shape[2], [(0, down, 0, fc, 0, down * fc, fc)], lon_ref.shape[0], turn)
    channels = x_hbm.shape[-1]
    copies[0].wait()
    split_rows((lat_ref, diag_ref), moved_rows(near, near_ref[...].reshape(-1, channels)))
    copies[1].wait()
    lon_ref[...] = moved_rows(far, far_ref[...].reshape(-1, channels)).astype(lon_ref.dtype)


def fine_first_kernel(
    plan, edge_ref, x_ref, gain_ref, w_ref, wo_ref, y_ref, *more
):
    rest_refs, (slat_ref, slon_ref, sdiag_ref, bias, qkv, att) = more[:-6], more[-6:]
    channels = x_ref.shape[1]
    levels, height, width = plan.levels, plan.height, plan.width
    fl, fc = HALF_LAT, HALF_LON
    turn = WIN_LEV // 2
    x = x_ref[...]
    count = plan.window
    area = WIN_LAT * WIN_LON
    block = y_ref.shape[0]

    def window_box(w, base):
        wr, wc = plan.windows[w]
        r0, c0 = fl + wr * WIN_LAT, fc + wc * WIN_LON
        return (r0, min(r0 + WIN_LAT, height), c0, min(c0 + WIN_LON, width), base, area, WIN_LON)

    tokens = moved_rows(box_hot(levels, height, width, [window_box(0, 0)], block, turn), x)
    normed = normed_rows(tokens, gain_ref[...])
    qkv[...] = jnp.dot(normed, w_ref[...], preferred_element_type=jnp.float32).astype(jnp.bfloat16)
    for w in range(1, len(plan.windows)):
        hot = box_hot(levels, height, width, [window_box(w, 0)], block, turn)
        rest_refs[w - 1][...] = moved_rows(hot, x).astype(jnp.bfloat16)
    for g in range(plan.groups):
        bias[2 * g] = score_bias(count, plan.group_split[g], 0)
        bias[2 * g + 1] = score_bias(count, plan.group_split[g], edge_ref[0])
    for pair in range(channels // LANES):
        for g in range(plan.groups):
            b = bias[2 * g] if plan.group_split[g] else None
            block_attention(qkv, att, g * count, channels, pair, b, count)
    update = jnp.dot(att[...], wo_ref[...], preferred_element_type=jnp.float32)
    y = (tokens + update).astype(jnp.bfloat16)
    y_ref[...] = y
    split_rows((slat_ref, slon_ref, sdiag_ref), moved_rows(sent_hot(plan, 0, sum(sent_sizes(plan))), y))


def sent_sizes(plan):
    return [plan.levels * len(cells) for cells in plan.results.values()]


def sent_hot(plan, w, out_rows, only=None):
    boxes, start = [], 0
    shifts = {"res_lat": (plan.height, 0), "res_lon": (0, plan.width), "res_diag": (plan.height, plan.width)}
    for name, cells in plan.results.items():
        sent = [cell for cell in shifted(cells, *shifts[name]) if cell is not None]
        r0, c0 = sent[0]
        r1, c1 = sent[-1]
        w0, v0 = plan.blocks[w][0]
        top, left = max(r0, w0), max(c0, v0)
        bottom, right = min(r1 + 1, w0 + WIN_LAT), min(c1 + 1, v0 + WIN_LON)
        if top < bottom and left < right and only in (None, name):
            row_step = c1 + 1 - c0
            base = start + (top - r0) * row_step + (left - c0)
            boxes.append((top - w0, bottom - w0, left - v0, right - v0, base, len(cells), row_step))
        if only is None:
            start += plan.levels * len(cells)
    if not boxes:
        return None
    return box_hot(plan.levels, WIN_LAT, WIN_LON, boxes, out_rows)


def raw_hot(plan, name, w, out_rows):
    cells = plan.raw[name]
    (r0, c0), (r1, c1) = cells[0], cells[-1]
    w0, v0 = plan.blocks[w][0]
    top, left = max(r0, w0), max(c0, v0)
    bottom, right = min(r1 + 1, w0 + WIN_LAT), min(c1 + 1, v0 + WIN_LON)
    if not (top < bottom and left < right):
        return None
    base = (top - w0) * WIN_LON + (left - v0)
    box = (top - r0, bottom - r0, left - c0, right - c0, base, WIN_LAT * WIN_LON, WIN_LON)
    return box_hot(plan.levels, r1 + 1 - r0, c1 + 1 - c0, [box], out_rows)


def fine_windows(plan, which, bias, rest_ref, raw, gain_ref, w_ref, wo_ref, y_ref, tokens, qkv, att):
    channels = rest_ref.shape[1]
    count = plan.window
    block = plan.groups * count
    for i, w in enumerate(which):
        value = rest_ref[i * block : (i + 1) * block, :].astype(jnp.float32)
        for name, ref in raw.items():
            hot = raw_hot(plan, name, w, block)
            if hot is not None:
                value = value + moved_rows(hot, ref[...])
        tokens[i * block : (i + 1) * block, :] = value
    normed = normed_rows(tokens[...], gain_ref[...])
    qkv[...] = jnp.dot(normed, w_ref[...], preferred_element_type=jnp.float32).astype(jnp.bfloat16)

    def window(i, below):
        for pair in range(channels // LANES):
            for g in range(plan.groups):
                row = i * block + g * count
                if not isinstance(row, int):
                    row = pl.multiple_of(row, 16)
                block_attention(qkv, att, row, channels, pair, bias[2 * g + below], count)

    belows = [plan.windows[w][0] for w in which]
    if len(which) == 1:
        window(0, belows[0])
    else:
        assert belows == list(range(len(which)))

        @pl.loop(0, len(which))
        def _(i):
            window(i, i)

    update = jnp.dot(att[...], wo_ref[...], preferred_element_type=jnp.float32)
    y = (tokens[...] + update).astype(jnp.bfloat16)
    y_ref[...] = y
    return y


def fine_edge_kernel(plan, w, name, raw_names, bias, sent_ref, rest_ref, *more):
    raw = dict(zip(raw_names, more))
    gain_ref, w_ref, wo_ref, y_ref, out_ref, tokens, qkv, att = more[len(raw_names) :]
    y = fine_windows(plan, [w], bias, rest_ref, raw, gain_ref, w_ref, wo_ref, y_ref, tokens, qkv, att)
    moved = moved_rows(sent_hot(plan, w, out_ref.shape[0], name), y)
    out_ref[...] = (sent_ref[...].astype(jnp.float32) + moved).astype(jnp.bfloat16)


def coarse_own_kernel(
    plan, keys, which, maps_ref, bias, first_ref, right_ref, below_ref, rest_ref, lat_ref, diag_ref, lon_ref, gain_ref, w_ref,
    wo_ref, part_ref, y_ref, tokens, qkv, att,
):
    raw = {"raw_lat": lat_ref, "raw_diag": diag_ref, "raw_lon": lon_ref}
    fine_windows(plan, which, bias, rest_ref, raw, gain_ref, w_ref, wo_ref, y_ref, tokens, qkv, att)
    area = WIN_LAT * WIN_LON
    hot = table_hot(maps_ref, keys["own"])
    total = part_ref.shape[0] // len(plan.parts)
    for i in range(plan.levels):
        rows = slice(i * area, (i + 1) * area)
        stacked = jnp.concatenate([ref[rows, :] for ref in (first_ref, right_ref, below_ref, y_ref)], 0)
        value = moved_rows(hot, stacked).astype(jnp.bfloat16)
        for k in range(len(plan.parts)):
            start = k * total + i * area
            part_ref[start : start + area, :] = value[k * area : (k + 1) * area]


def thirds(value):
    first = value.astype(jnp.bfloat16).astype(jnp.float32)
    second = (value - first).astype(jnp.bfloat16).astype(jnp.float32)
    return jnp.concatenate([first, second, value - first - second], 0).astype(jnp.bfloat16)


def summed_thirds(stacked, right):
    out = jnp.dot(stacked, right, preferred_element_type=jnp.float32)
    rows = out.shape[0] // 3
    return out[:rows] + out[rows : 2 * rows] + out[2 * rows :]


def coarse_kernel(
    plan, keys, maps_ref, bias, part_ref, lat_ref, lon_ref, diag_ref, gm_ref, wm_ref, gs_ref, ws_ref, wo_ref,
    wsp_ref, lat_index_ref, weight_ref, fine_ref, upper_ref, sums_ref, qkv, att,
):
    parts = len(plan.parts)
    channels = part_ref.shape[1]
    total = upper_ref.shape[0]
    wide = ws_ref.shape[0]
    count = plan.window
    levels = plan.levels
    area = total // levels
    hot = table_hot(maps_ref, keys["ahead"])
    for i in range(levels):
        pieces = []
        for ref in (lat_ref, lon_ref, diag_ref):
            size = ref.shape[0] // levels
            pieces.append(ref[i * size : (i + 1) * size, :])
        value = moved_rows(hot, jnp.concatenate(pieces, 0))
        for k in range(parts):
            rows = slice(k * total + i * area, k * total + (i + 1) * area)
            own = part_ref[rows, :].astype(jnp.float32)
            fine_ref[rows, :] = (own + value[k * area : (k + 1) * area]).astype(jnp.bfloat16)

    def part(k):
        return fine_ref[k * total : (k + 1) * total, :].astype(jnp.float32)

    mean = sum(jnp.sum(part(k), -1, keepdims=True) for k in range(parts)) / (parts * channels)
    square = sum(jnp.sum((part(k) - mean) ** 2, -1, keepdims=True) for k in range(parts))
    scale = lax.rsqrt(square / (parts * channels) + epsilon)
    merged = 0.0
    for k in range(parts):
        span = slice(k * channels, (k + 1) * channels)
        normed = ((part(k) - mean) * scale * gm_ref[:, span]).astype(jnp.bfloat16)
        merged = merged + jnp.dot(normed, wm_ref[span, :], preferred_element_type=jnp.float32)
    coarse = merged.astype(jnp.bfloat16).astype(jnp.float32)
    normed = normed_rows(coarse, gs_ref[...])
    qkv[...] = jnp.dot(normed, ws_ref[...], preferred_element_type=jnp.float32).astype(jnp.bfloat16)

    at_once = 8

    @pl.loop(0, wide // LANES // at_once)
    def _(step):
        for i in range(at_once):
            for g in range(plan.groups):
                block_attention(qkv, att, g * count, wide, step * at_once + i, bias[2 * g + 1], count)

    update = jnp.dot(att[...], wo_ref[...], preferred_element_type=jnp.float32)
    upper = (coarse + update).astype(jnp.bfloat16)
    upper_ref[...] = upper
    span = total // levels
    token = lax.broadcasted_iota(jnp.int32, (levels, total), 1)
    level = lax.broadcasted_iota(jnp.int32, (levels, total), 0)
    inside = (token >= level * span) & (token < (level + 1) * span)
    mine = weight_ref[lat_index_ref[0]]
    rows = jnp.concatenate([jnp.where(inside, mine[ro : ro + 1, :], 0.0) for ro in range(2)], 0)
    weights = thirds(rows)
    heavy = thirds(summed_thirds(weights, upper))
    spread = summed_thirds(heavy, wsp_ref[...])
    sums = 0.0
    for k in range(parts):
        ro = k // 2
        fine = summed_thirds(weights, fine_ref[k * total : (k + 1) * total, :])
        sums = sums + (fine + spread[:, k * channels : (k + 1) * channels])[ro * levels : (ro + 1) * levels]
    for i, lv in enumerate(plan.order):
        sums_ref[lv : lv + 1, :] = sums[i : i + 1]


def split_kernel(plan, keys, maps_ref, fine_ref, upper_ref, wsp_ref, own_ref, slat_ref, slon_ref, sdiag_ref, decoded):
    parts = len(plan.parts)
    total = upper_ref.shape[0]
    channels = fine_ref.shape[1]
    levels = plan.levels
    span = total // levels
    upper = upper_ref[...]
    for k in range(parts):
        spread = jnp.dot(upper, wsp_ref[:, k * channels : (k + 1) * channels], preferred_element_type=jnp.float32)
        value = (fine_ref[k * total : (k + 1) * total, :].astype(jnp.float32) + spread).astype(jnp.bfloat16)
        for i in range(levels):
            decoded[i, k * span : (k + 1) * span, :] = value[i * span : (i + 1) * span]
    quarter = parts * (span // 4)
    hot = table_hot(maps_ref, keys["quarters"])
    for i in range(levels):
        moved = jnp.dot(hot, decoded[i], preferred_element_type=jnp.float32).astype(jnp.bfloat16)
        for q, out in enumerate((own_ref, slon_ref, slat_ref, sdiag_ref)):
            out[i * quarter : (i + 1) * quarter, :] = moved[q * quarter : (q + 1) * quarter]


def output_kernel(
    plan, keys, maps_ref, own_ref, lon_ref, lat_ref, diag_ref, sums_ref, other_ref, out_ref, means_ref
):
    means_ref[...] = sums_ref[...] + other_ref[...]
    span = own_ref.shape[0] // plan.levels
    tile = plan.height * plan.width
    hot = table_hot(maps_ref, keys["output"])
    for i, lv in enumerate(plan.order):
        rows = slice(i * span, (i + 1) * span)
        stacked = jnp.concatenate(
            [ref[rows, :].astype(jnp.float32) for ref in (own_ref, lon_ref, lat_ref, diag_ref)], 0
        ).astype(jnp.bfloat16)
        moved = jnp.dot(hot, stacked, preferred_element_type=jnp.float32)
        out_ref[lv * tile : (lv + 1) * tile, :] = moved.astype(jnp.bfloat16)


def all_but_summed(value):
    steps = {}
    for axis in ("lat", "lon"):
        count = lax.axis_size(axis)
        assert count & (count - 1) == 0
        steps[axis] = [(axis, 1 << i) for i in range(count.bit_length() - 1)]
    order = steps["lat"][:1] + steps["lon"][1:] + steps["lon"][:1] + steps["lat"][1:]
    other = jnp.zeros_like(value)
    for number, (axis, step) in enumerate(order):
        value = value if number == 0 else value + other
        other = lax.ppermute(value, axis, [(i, i ^ step) for i in range(lax.axis_size(axis))])
    return value, other


def whole_step(
    latent, gain_first, triple_first, output_first, gain_merge, merge_weight, gain_second, triple_second,
    output_second, split_weight,
):
    levels, height, width, channels = latent.shape
    wide = merge_weight.shape[1]
    plan = Plan(levels, height, width)
    maps = Maps()
    lat_count, lon_count = lax.axis_size("lat"), lax.axis_size("lon")

    def moved(value, lat_step, lon_step):
        pairs = [
            (a * lon_count + b, (a + lat_step) % lat_count * lon_count + (b + lon_step) % lon_count)
            for a in range(lat_count)
            for b in range(lon_count)
        ]
        return lax.ppermute(value, ("lat", "lon"), pairs)

    all_parts = sum(plan.parts, [])
    maps.add("own", sum(plan.blocks, []), all_parts)
    maps.add("ahead", sum(plan.results.values(), []), all_parts)
    cells = [
        (2 * r + ro, 2 * c + co)
        for ro in range(2)
        for co in range(2)
        for r in range(plan.coarse_rows)
        for c in range(plan.coarse_cols)
    ]
    half_rows, half_cols = height // 2, width // 2
    quarters = [
        (qr * half_rows + r, qc * half_cols + c)
        for qr in range(2)
        for qc in range(2)
        for r in range(half_rows)
        for c in range(half_cols)
    ]
    maps.add("quarters", cells, quarters)
    placed = [((r + half_rows) % height, (c + half_cols) % width) for r, c in quarters]
    maps.add("output", placed, plan.own)
    table, keys = maps.array(), maps.keys

    vmem = pl.BlockSpec(memory_space=pltpu.VMEM)
    smem = pl.BlockSpec(memory_space=pltpu.SMEM)
    bf16 = jnp.bfloat16

    def call(body, outs, args, scratch=(), flops=0, limit=16, specs=None):
        size = sum(math.prod(a.shape) * a.dtype.itemsize for a in args)
        return pl.pallas_call(
            body,
            out_shape=[jax.ShapeDtypeStruct(s, d) for s, d in outs],
            in_specs=specs or [smem if a.ndim == 1 else vmem for a in args],
            out_specs=[vmem] * len(outs),
            scratch_shapes=list(scratch),
            cost_estimate=pl.CostEstimate(flops=flops, bytes_accessed=size, transcendentals=0),
            compiler_params=pltpu.CompilerParams(vmem_limit_bytes=limit << 20),
        )(*args)

    def rows_of(*counts):
        return [((n, channels), bf16) for n in counts]

    count = plan.window
    x = latent.reshape(levels * height * width, channels)
    lat_index = lax.axis_index("lat").astype(jnp.int32)
    edge = (lat_index == lat_count - 1).astype(jnp.int32).reshape(1)
    n_block = plan.groups * count
    n_coarse = levels * len(plan.parts[0])
    n_part = len(plan.parts)
    n_sent = sent_sizes(plan)

    hbm = pl.BlockSpec(memory_space=pltpu.HBM)
    margin = -(-HALF_LON // 8) * 8
    s_lat, s_diag, s_lon = call(
        functools.partial(pack_kernel, plan),
        rows_of(*[levels * len(cells) for cells in plan.raw.values()]), (latent,),
        [
            pltpu.VMEM((levels, HALF_LAT, width, channels), bf16),
            pltpu.VMEM((levels, height - HALF_LAT, margin, channels), bf16),
            pltpu.SemaphoreType.DMA((2,)),
        ],
        flops=10**9, limit=LIMITS["pack"], specs=[hbm],
    )
    r_lat = moved(s_lat, -1, 0)
    r_diag = moved(s_diag, -1, -1)
    r_lon = moved(s_lon, 0, -1)
    gain1 = gain_first.reshape(1, channels)
    y_first, x_right, x_below, x_last, s_lat, s_lon, s_diag, bias = call(
        functools.partial(fine_first_kernel, plan),
        rows_of(n_block, *[n_block] * (len(plan.windows) - 1), *n_sent)
        + [((2 * plan.groups, count, count), jnp.float32)],
        (edge, x, gain1, triple_first, output_first),
        [pltpu.VMEM((n_block, 3 * channels), bf16), pltpu.VMEM((n_block, channels), bf16)],
        flops=4 * 10**9, limit=LIMITS["first"],
    )
    fine_scratch = [
        pltpu.VMEM((n_block, channels), jnp.float32),
        pltpu.VMEM((n_block, 3 * channels), bf16),
        pltpu.VMEM((n_block, channels), bf16),
    ]
    fine_weights = (gain1, triple_first, output_first)

    def fine_edge(w, direction, sent, rest, raws):
        return call(
            functools.partial(fine_edge_kernel, plan, w, direction, list(raws)),
            rows_of(n_block, sent.shape[0]), (bias, sent, rest, *raws.values(), *fine_weights),
            fine_scratch, flops=2 * 10**9, limit=LIMITS["edge"],
        )

    y_right, s_lat = fine_edge(1, "res_lat", s_lat, x_right, {"raw_lon": r_lon})
    q_lat = moved(s_lat, -1, 0)
    q_diag = moved(s_diag, -1, -1)
    y_below, s_lon = fine_edge(2, "res_lon", s_lon, x_below, {"raw_lat": r_lat})
    q_lon = moved(s_lon, 0, -1)
    (parts,) = call(
        functools.partial(coarse_own_kernel, plan, keys, [len(plan.windows) - 1]),
        rows_of(n_part * n_coarse),
        (table, bias, y_first, y_right, y_below, x_last, r_lat, r_diag, r_lon, *fine_weights),
        [pltpu.VMEM((n_block, channels), bf16)] + fine_scratch, flops=4 * 10**9, limit=LIMITS["own"],
    )
    total_rows, total_cols = height * lat_count, width * lon_count
    angle = np.pi * ((np.arange(total_rows) + 0.5) / total_rows - 0.5)
    every = np.cos(angle)
    scaled = every / np.sqrt(total_cols * np.sum(every * every))
    frame_rows = np.array([[r for r, _ in plan.parts[2 * ro]] * levels for ro in range(2)])
    row_of = (np.arange(lat_count)[:, None, None] * height + frame_rows) % total_rows
    weights = jnp.asarray(scaled[row_of], jnp.float32)
    fine, upper, sums = call(
        functools.partial(coarse_kernel, plan, keys),
        rows_of(n_part * n_coarse) + [((n_coarse, wide), bf16), ((levels, channels), jnp.float32)],
        (
            table, bias, parts, q_lat, q_lon, q_diag, gain_merge.reshape(1, -1), merge_weight,
            gain_second.reshape(1, -1), triple_second, output_second, split_weight, lat_index.reshape(1), weights,
        ),
        [pltpu.VMEM((n_coarse, 3 * wide), bf16), pltpu.VMEM((n_coarse, wide), bf16)],
        flops=8 * 10**9, limit=LIMITS["coarse"],
    )
    own, s_lat, s_lon, s_diag = call(
        functools.partial(split_kernel, plan, keys), rows_of(*[n_coarse] * 4),
        (table, fine, upper, split_weight), [pltpu.VMEM((levels, n_part * n_coarse // levels, channels), bf16)],
        flops=2 * 10**9, limit=LIMITS["split"],
    )
    d_lat, d_lon, d_diag = (moved(s_lat, 1, 0), moved(s_lon, 0, 1), moved(s_diag, 1, 1))
    sums, other_sums = all_but_summed(sums)
    decoded, means = call(
        functools.partial(output_kernel, plan, keys),
        rows_of(levels * height * width) + [((levels, channels), jnp.float32)],
        (table, own, d_lon, d_lat, d_diag, sums, other_sums), flops=10**9, limit=LIMITS["output"],
    )
    return decoded.reshape(latent.shape), means


def solution(mesh):
    return jax.shard_map(
        whole_step,
        mesh=mesh,
        in_specs=(P(None, "lat", "lon", None), P(), P(), P(), P(), P(), P(), P(), P(), P()),
        out_specs=(P(None, "lat", "lon", None), P()),
        check_vma=False,
    )
```

```python
import functools
import math

import jax
import jax.numpy as jnp
import numpy as np
from jax import lax
from jax.experimental import pallas as pl
from jax.experimental.pallas import tpu as pltpu
from jax.sharding import PartitionSpec as P

HD = 64
WIN_LEV = 2
WIN_LAT = 6
WIN_LON = 12
HALF_LAT = WIN_LAT // 2
HALF_LON = WIN_LON // 2
LANES = 128

epsilon = 1e-05
masked_score = -1e30
score_scale = HD**-0.5 * math.log2(math.e)

LIMITS = {"pack": 59, "first": 16, "edge": 16, "own": 12, "coarse": 16, "split": 8, "output": 8}


class Plan:
    def __init__(self, levels, height, width):
        self.levels, self.height, self.width = levels, height, width
        assert levels % WIN_LEV == 0
        assert height == 2 * WIN_LAT and width == 2 * WIN_LON
        self.groups = levels // WIN_LEV
        half_lev = WIN_LEV // 2
        self.group_levels = [
            [(g * WIN_LEV + half_lev + i) % levels for i in range(WIN_LEV)] for g in range(self.groups)
        ]
        self.order = [lv for group in self.group_levels for lv in group]
        ids = [(((lv + half_lev)) // WIN_LEV) for lv in range(levels)]
        self.group_split = [len({ids[lv] for lv in group}) > 1 for group in self.group_levels]
        self.window = WIN_LEV * WIN_LAT * WIN_LON
        self.windows = [(wr, wc) for wr in range(height // WIN_LAT) for wc in range(width // WIN_LON)]

        self.blocks = [
            cells_of(
                (HALF_LAT + wr * WIN_LAT, HALF_LAT + (wr + 1) * WIN_LAT),
                (HALF_LON + wc * WIN_LON, HALF_LON + (wc + 1) * WIN_LON),
            )
            for wr, wc in self.windows
        ]
        self.own = cells_of((0, height), (0, width))
        fl, fc, fh, fw = HALF_LAT, HALF_LON, height, width
        self.raw = {
            "raw_lat": cells_of((fh, fh + fl), (fc, fw)),
            "raw_diag": cells_of((fh, fh + fl), (fw, fw + fc)),
            "raw_lon": cells_of((fl, fh), (fw, fw + fc)),
        }
        self.results = {
            "res_lat": padded(cells_of((fh + fl, fh + 2 * fl), (2 * fc, fw + fc))),
            "res_lon": padded(cells_of((2 * fl, fh + fl), (fw + fc, fw + 2 * fc))),
            "res_diag": padded(cells_of((fh + fl, fh + 2 * fl), (fw + fc, fw + 2 * fc))),
        }
        self.coarse_rows, self.coarse_cols = height // 2, width // 2
        self.parts = [
            [
                (2 * fl + 2 * r + ro, 2 * fc + 2 * c + co)
                for r in range(self.coarse_rows)
                for c in range(self.coarse_cols)
            ]
            for ro in range(2)
            for co in range(2)
        ]


def cells_of(rows, cols):
    return [(r, c) for r in range(*rows) for c in range(*cols)]


def padded(cells):
    return cells + [None] * (-len(cells) % 8)


def shifted(cells, rows, cols):
    return [cell and (cell[0] - rows, cell[1] - cols) for cell in cells]


def scatter_map(source, target):
    place = {cell: i for i, cell in enumerate(target) if cell is not None}
    return np.array([-1 if cell is None else place.get(cell, -1) for cell in source], np.int32)


class Maps:
    def __init__(self):
        self.rows, self.keys = [], {}

    def add(self, key, source, target):
        self.keys[key] = (len(self.rows), len(source), len(target))
        self.rows.append(scatter_map(source, target))

    def array(self):
        width = -(-max(len(v) for v in self.rows) // LANES) * LANES
        height = -(-len(self.rows) // 8) * 8
        out = np.full((height, width), -1, np.int32)
        for i, v in enumerate(self.rows):
            out[i, : len(v)] = v
        return jnp.asarray(out)


def table_hot(maps_ref, key):
    row, count, out_rows = key
    return one_hot(maps_ref[row : row + 1, :count], out_rows)


def one_hot(index, out_rows):
    hot = lax.broadcasted_iota(jnp.int32, (out_rows, index.shape[1]), 0) == index
    return jnp.where(hot, 1.0, 0.0).astype(jnp.bfloat16)


def box_hot(levels, rows, cols, boxes, out_rows, turn=0):
    token = lax.broadcasted_iota(jnp.int32, (1, levels * rows * cols), 1)

    def divided(value, by):
        return jnp.floor((value.astype(jnp.float32) + 0.5) * (1.0 / by)).astype(jnp.int32)

    level = divided(token, rows * cols)
    inner = token - level * (rows * cols)
    row = divided(inner, cols)
    col = inner - row * cols
    slot = jnp.where(level >= turn, level - turn, level + levels - turn)
    place = jnp.full_like(token, -1)
    for r0, r1, c0, c1, base, level_step, row_step in boxes:
        inside = (row >= r0) & (row < r1) & (col >= c0) & (col < c1)
        place = jnp.where(inside, base + slot * level_step + (row - r0) * row_step + (col - c0), place)
    return one_hot(place, out_rows)


def moved_rows(hot, source):
    return jnp.dot(hot, source, preferred_element_type=jnp.float32)


def normed_rows(value, gain):
    mean = jnp.mean(value, -1, keepdims=True)
    centred = value - mean
    var = jnp.mean(centred * centred, -1, keepdims=True)
    return (centred * lax.rsqrt(var + epsilon) * gain).astype(jnp.bfloat16)


def score_bias(count, group_split, edge):
    span = count // WIN_LEV
    rows = lax.broadcasted_iota(jnp.int32, (count, count), 0)
    cols = lax.broadcasted_iota(jnp.int32, (count, count), 1)
    q_lev, k_lev = rows >= span, cols >= span
    q_in = rows - jnp.where(q_lev, span, 0)
    k_in = cols - jnp.where(k_lev, span, 0)
    half = span // 2
    apart = (q_in >= half) != (k_in >= half)
    apart = jnp.where(apart, edge, 0)
    if group_split:
        apart = jnp.where(q_lev != k_lev, 1, apart)
    return jnp.where(apart > 0, masked_score, 0.0)


def head_pair(q, k, v, bias, low, high):
    trans = (((1,), (1,)), ((), ()))
    outs = []
    for keep, fill in ((low, high), (high, low)):
        s = lax.dot_general(q, k * keep, trans, preferred_element_type=jnp.float32)
        if bias is not None:
            s = s + bias
        peak = jnp.max(s, -1, keepdims=True)
        p = jnp.exp2((s - peak) * score_scale).astype(jnp.bfloat16)
        outs.append(jnp.dot(p, v * keep + fill, preferred_element_type=jnp.float32))
    is_low = lax.broadcasted_iota(jnp.int32, outs[0].shape, 1) < HD
    top = jnp.where(is_low, outs[0], outs[1])
    bottom = pltpu.roll(jnp.where(is_low, outs[1], outs[0]), HD, 1)
    return (top / bottom).astype(jnp.bfloat16)


def lane_masks():
    lane = lax.broadcasted_iota(jnp.int32, (1, LANES), 1)
    low = jnp.where(lane < HD, 1.0, 0.0).astype(jnp.bfloat16)
    high = jnp.where(lane < HD, 0.0, 1.0).astype(jnp.bfloat16)
    return low, high


def block_attention(qkv, att, row, channels, pair, bias, count):
    low, high = lane_masks()
    rows = pl.ds(row, count)
    base = pair * LANES

    def lanes(offset):
        start = base + offset
        return pl.ds(start if isinstance(start, int) else pl.multiple_of(start, LANES), LANES)

    q = qkv[rows, lanes(0)]
    k = qkv[rows, lanes(channels)]
    v = qkv[rows, lanes(2 * channels)]
    att[rows, lanes(0)] = head_pair(q, k, v, bias, low, high)


def split_rows(out_refs, value):
    start = 0
    for out in out_refs:
        out[...] = value[start : start + out.shape[0]].astype(out.dtype)
        start += out.shape[0]


def pack_kernel(plan, x_hbm, lat_ref, diag_ref, lon_ref, near_ref, far_ref, sems):
    levels, height, width = plan.levels, plan.height, plan.width
    fl, fc = HALF_LAT, HALF_LON
    copies = [
        pltpu.make_async_copy(x_hbm.at[:, 0:fl], near_ref, sems.at[0]),
        pltpu.make_async_copy(x_hbm.at[:, fl:height, 0 : far_ref.shape[2]], far_ref, sems.at[1]),
    ]
    for copy in copies:
        copy.start()
    turn = WIN_LEV // 2
    across, down = width - fc, height - fl
    lat_size, diag_size = lat_ref.shape[0], diag_ref.shape[0]
    near = box_hot(
        levels, fl, width,
        [(0, fl, fc, width, 0, fl * across, across), (0, fl, 0, fc, lat_size, fl * fc, fc)],
        lat_size + diag_size, turn,
    )
    far = box_hot(levels, down, far_ref.shape[2], [(0, down, 0, fc, 0, down * fc, fc)], lon_ref.shape[0], turn)
    channels = x_hbm.shape[-1]
    copies[0].wait()
    split_rows((lat_ref, diag_ref), moved_rows(near, near_ref[...].reshape(-1, channels)))
    copies[1].wait()
    lon_ref[...] = moved_rows(far, far_ref[...].reshape(-1, channels)).astype(lon_ref.dtype)


def fine_first_kernel(
    plan, edge_ref, x_ref, gain_ref, w_ref, wo_ref, y_ref, *more
):
    rest_refs, (slat_ref, slon_ref, sdiag_ref, bias, qkv, att, tokens_ref) = more[:-7], more[-7:]
    channels = x_ref.shape[1]
    levels, height, width = plan.levels, plan.height, plan.width
    fl, fc = HALF_LAT, HALF_LON
    count = plan.window
    area = WIN_LAT * WIN_LON

    def level_hot(rows):
        boxes = [
            (0, rows, fc, fc + WIN_LON, 0, 0, WIN_LON),
            (0, rows, fc + WIN_LON, width, area, 0, WIN_LON),
        ]
        return box_hot(1, rows, width, boxes, 2 * area)

    split_row = fl + WIN_LAT
    top_hot, bottom_hot = level_hot(WIN_LAT), level_hot(height - split_row)
    right_ref, below_ref, last_ref = rest_refs
    for i, lv in enumerate(plan.order):
        start = lv * height * width
        rows = slice(i * area, (i + 1) * area)
        top = moved_rows(top_hot, x_ref[start + fl * width : start + split_row * width, :])
        tokens_ref[rows, :] = top[:area]
        right_ref[rows, :] = top[area:].astype(jnp.bfloat16)
        bottom = moved_rows(bottom_hot, x_ref[start + split_row * width : start + height * width, :])
        below_ref[rows, :] = bottom[:area].astype(jnp.bfloat16)
        last_ref[rows, :] = bottom[area:].astype(jnp.bfloat16)
    tokens = tokens_ref[...]
    normed = normed_rows(tokens, gain_ref[...])
    qkv[...] = jnp.dot(normed, w_ref[...], preferred_element_type=jnp.float32).astype(jnp.bfloat16)
    for g in range(plan.groups):
        bias[2 * g] = score_bias(count, plan.group_split[g], 0)
        bias[2 * g + 1] = score_bias(count, plan.group_split[g], edge_ref[0])
    for pair in range(channels // LANES):
        for g in range(plan.groups):
            b = bias[2 * g] if plan.group_split[g] else None
            block_attention(qkv, att, g * count, channels, pair, b, count)
    update = jnp.dot(att[...], wo_ref[...], preferred_element_type=jnp.float32)
    y = (tokens + update).astype(jnp.bfloat16)
    y_ref[...] = y
    hot = sent_hot(plan, 0)
    for i in range(levels):
        moved = moved_rows(hot, y_ref[i * area : (i + 1) * area, :]).astype(jnp.bfloat16)
        start = 0
        for out in (slat_ref, slon_ref, sdiag_ref):
            size = out.shape[0] // levels
            out[i * size : (i + 1) * size, :] = moved[start : start + size]
            start += size


def sent_sizes(plan):
    return [plan.levels * len(cells) for cells in plan.results.values()]


def sent_hot(plan, w, only=None):
    boxes, start = [], 0
    shifts = {"res_lat": (plan.height, 0), "res_lon": (0, plan.width), "res_diag": (plan.height, plan.width)}
    for name, cells in plan.results.items():
        sent = [cell for cell in shifted(cells, *shifts[name]) if cell is not None]
        r0, c0 = sent[0]
        r1, c1 = sent[-1]
        w0, v0 = plan.blocks[w][0]
        top, left = max(r0, w0), max(c0, v0)
        bottom, right = min(r1 + 1, w0 + WIN_LAT), min(c1 + 1, v0 + WIN_LON)
        if top < bottom and left < right and only in (None, name):
            row_step = c1 + 1 - c0
            base = start + (top - r0) * row_step + (left - c0)
            boxes.append((top - w0, bottom - w0, left - v0, right - v0, base, len(cells), row_step))
        if only is None:
            start += len(cells)
    out_rows = start if only is None else len(plan.results[only])
    return box_hot(1, WIN_LAT, WIN_LON, boxes, out_rows)


def raw_hot(plan, name, w, out_rows):
    cells = plan.raw[name]
    (r0, c0), (r1, c1) = cells[0], cells[-1]
    w0, v0 = plan.blocks[w][0]
    top, left = max(r0, w0), max(c0, v0)
    bottom, right = min(r1 + 1, w0 + WIN_LAT), min(c1 + 1, v0 + WIN_LON)
    if not (top < bottom and left < right):
        return None
    base = (top - w0) * WIN_LON + (left - v0)
    box = (top - r0, bottom - r0, left - c0, right - c0, base, WIN_LAT * WIN_LON, WIN_LON)
    return box_hot(plan.levels, r1 + 1 - r0, c1 + 1 - c0, [box], out_rows)


def fine_windows(plan, which, bias, rest_ref, raw, gain_ref, w_ref, wo_ref, y_ref, tokens, qkv, att):
    channels = rest_ref.shape[1]
    count = plan.window
    block = plan.groups * count
    for i, w in enumerate(which):
        value = rest_ref[i * block : (i + 1) * block, :].astype(jnp.float32)
        for name, ref in raw.items():
            hot = raw_hot(plan, name, w, block)
            if hot is not None:
                value = value + moved_rows(hot, ref[...])
        tokens[i * block : (i + 1) * block, :] = value
    normed = normed_rows(tokens[...], gain_ref[...])
    qkv[...] = jnp.dot(normed, w_ref[...], preferred_element_type=jnp.float32).astype(jnp.bfloat16)

    def window(i, below):
        for pair in range(channels // LANES):
            for g in range(plan.groups):
                row = i * block + g * count
                if not isinstance(row, int):
                    row = pl.multiple_of(row, 16)
                block_attention(qkv, att, row, channels, pair, bias[2 * g + below], count)

    belows = [plan.windows[w][0] for w in which]
    if len(which) == 1:
        window(0, belows[0])
    else:
        assert belows == list(range(len(which)))

        @pl.loop(0, len(which))
        def _(i):
            window(i, i)

    update = jnp.dot(att[...], wo_ref[...], preferred_element_type=jnp.float32)
    y = (tokens[...] + update).astype(jnp.bfloat16)
    y_ref[...] = y
    return y


def fine_edge_kernel(plan, w, name, raw_names, bias, sent_ref, rest_ref, *more):
    raw = dict(zip(raw_names, more))
    gain_ref, w_ref, wo_ref, y_ref, out_ref, tokens, qkv, att = more[len(raw_names) :]
    fine_windows(plan, [w], bias, rest_ref, raw, gain_ref, w_ref, wo_ref, y_ref, tokens, qkv, att)
    hot = sent_hot(plan, w, name)
    area, size = WIN_LAT * WIN_LON, out_ref.shape[0] // plan.levels
    for i in range(plan.levels):
        rows = slice(i * size, (i + 1) * size)
        moved = moved_rows(hot, y_ref[i * area : (i + 1) * area, :])
        out_ref[rows, :] = (sent_ref[rows, :].astype(jnp.float32) + moved).astype(jnp.bfloat16)


def coarse_own_kernel(
    plan, keys, which, maps_ref, bias, first_ref, right_ref, below_ref, rest_ref, lat_ref, diag_ref, lon_ref, gain_ref, w_ref,
    wo_ref, part_ref, y_ref, tokens, qkv, att,
):
    raw = {"raw_lat": lat_ref, "raw_diag": diag_ref, "raw_lon": lon_ref}
    fine_windows(plan, which, bias, rest_ref, raw, gain_ref, w_ref, wo_ref, y_ref, tokens, qkv, att)
    area = WIN_LAT * WIN_LON
    hot = table_hot(maps_ref, keys["own"])
    total = part_ref.shape[0] // len(plan.parts)
    for i in range(plan.levels):
        rows = slice(i * area, (i + 1) * area)
        stacked = jnp.concatenate([ref[rows, :] for ref in (first_ref, right_ref, below_ref, y_ref)], 0)
        value = moved_rows(hot, stacked).astype(jnp.bfloat16)
        for k in range(len(plan.parts)):
            start = k * total + i * area
            part_ref[start : start + area, :] = value[k * area : (k + 1) * area]


def thirds(value):
    first = value.astype(jnp.bfloat16).astype(jnp.float32)
    second = (value - first).astype(jnp.bfloat16).astype(jnp.float32)
    return jnp.concatenate([first, second, value - first - second], 0).astype(jnp.bfloat16)


def summed_thirds(stacked, right):
    out = jnp.dot(stacked, right, preferred_element_type=jnp.float32)
    rows = out.shape[0] // 3
    return out[:rows] + out[rows : 2 * rows] + out[2 * rows :]


def coarse_kernel(
    plan, keys, maps_ref, bias, part_ref, lat_ref, lon_ref, diag_ref, gm_ref, wm_ref, gs_ref, ws_ref, wo_ref,
    wsp_ref, lat_index_ref, weight_ref, fine_ref, upper_ref, sums_ref, qkv, att,
):
    parts = len(plan.parts)
    channels = part_ref.shape[1]
    total = upper_ref.shape[0]
    wide = ws_ref.shape[0]
    count = plan.window
    levels = plan.levels
    area = total // levels
    hot = table_hot(maps_ref, keys["ahead"])
    for i in range(levels):
        pieces = []
        for ref in (lat_ref, lon_ref, diag_ref):
            size = ref.shape[0] // levels
            pieces.append(ref[i * size : (i + 1) * size, :])
        value = moved_rows(hot, jnp.concatenate(pieces, 0))
        for k in range(parts):
            rows = slice(k * total + i * area, k * total + (i + 1) * area)
            own = part_ref[rows, :].astype(jnp.float32)
            fine_ref[rows, :] = (own + value[k * area : (k + 1) * area]).astype(jnp.bfloat16)

    def part(k):
        return fine_ref[k * total : (k + 1) * total, :].astype(jnp.float32)

    mean = sum(jnp.sum(part(k), -1, keepdims=True) for k in range(parts)) / (parts * channels)
    square = sum(jnp.sum((part(k) - mean) ** 2, -1, keepdims=True) for k in range(parts))
    scale = lax.rsqrt(square / (parts * channels) + epsilon)
    merged = 0.0
    for k in range(parts):
        span = slice(k * channels, (k + 1) * channels)
        normed = ((part(k) - mean) * scale * gm_ref[:, span]).astype(jnp.bfloat16)
        merged = merged + jnp.dot(normed, wm_ref[span, :], preferred_element_type=jnp.float32)
    coarse = merged.astype(jnp.bfloat16).astype(jnp.float32)
    normed = normed_rows(coarse, gs_ref[...])
    qkv[...] = jnp.dot(normed, ws_ref[...], preferred_element_type=jnp.float32).astype(jnp.bfloat16)

    at_once = 8

    @pl.loop(0, wide // LANES // at_once)
    def _(step):
        for i in range(at_once):
            for g in range(plan.groups):
                block_attention(qkv, att, g * count, wide, step * at_once + i, bias[2 * g + 1], count)

    update = jnp.dot(att[...], wo_ref[...], preferred_element_type=jnp.float32)
    upper = (coarse + update).astype(jnp.bfloat16)
    upper_ref[...] = upper
    span = total // levels
    token = lax.broadcasted_iota(jnp.int32, (levels, total), 1)
    level = lax.broadcasted_iota(jnp.int32, (levels, total), 0)
    inside = (token >= level * span) & (token < (level + 1) * span)
    mine = weight_ref[lat_index_ref[0]]
    rows = jnp.concatenate([jnp.where(inside, mine[ro : ro + 1, :], 0.0) for ro in range(2)], 0)
    weights = thirds(rows)
    heavy = thirds(summed_thirds(weights, upper))
    spread = summed_thirds(heavy, wsp_ref[...])
    sums = 0.0
    for k in range(parts):
        ro = k // 2
        fine = summed_thirds(weights, fine_ref[k * total : (k + 1) * total, :])
        sums = sums + (fine + spread[:, k * channels : (k + 1) * channels])[ro * levels : (ro + 1) * levels]
    for i, lv in enumerate(plan.order):
        sums_ref[lv : lv + 1, :] = sums[i : i + 1]


def split_kernel(plan, keys, maps_ref, fine_ref, upper_ref, wsp_ref, own_ref, slat_ref, slon_ref, sdiag_ref, decoded):
    parts = len(plan.parts)
    total = upper_ref.shape[0]
    channels = fine_ref.shape[1]
    levels = plan.levels
    span = total // levels
    upper = upper_ref[...]
    for k in range(parts):
        spread = jnp.dot(upper, wsp_ref[:, k * channels : (k + 1) * channels], preferred_element_type=jnp.float32)
        value = (fine_ref[k * total : (k + 1) * total, :].astype(jnp.float32) + spread).astype(jnp.bfloat16)
        for i in range(levels):
            decoded[i, k * span : (k + 1) * span, :] = value[i * span : (i + 1) * span]
    quarter = parts * (span // 4)
    hot = table_hot(maps_ref, keys["quarters"])
    for i in range(levels):
        moved = jnp.dot(hot, decoded[i], preferred_element_type=jnp.float32).astype(jnp.bfloat16)
        for q, out in enumerate((own_ref, slon_ref, slat_ref, sdiag_ref)):
            out[i * quarter : (i + 1) * quarter, :] = moved[q * quarter : (q + 1) * quarter]


def output_kernel(
    plan, keys, maps_ref, own_ref, lon_ref, lat_ref, diag_ref, sums_ref, other_ref, out_ref, means_ref
):
    means_ref[...] = sums_ref[...] + other_ref[...]
    span = own_ref.shape[0] // plan.levels
    tile = plan.height * plan.width
    hot = table_hot(maps_ref, keys["output"])
    for i, lv in enumerate(plan.order):
        rows = slice(i * span, (i + 1) * span)
        stacked = jnp.concatenate(
            [ref[rows, :].astype(jnp.float32) for ref in (own_ref, lon_ref, lat_ref, diag_ref)], 0
        ).astype(jnp.bfloat16)
        moved = jnp.dot(hot, stacked, preferred_element_type=jnp.float32)
        out_ref[lv * tile : (lv + 1) * tile, :] = moved.astype(jnp.bfloat16)


def all_but_summed(value):
    steps = {}
    for axis in ("lat", "lon"):
        count = lax.axis_size(axis)
        assert count & (count - 1) == 0
        steps[axis] = [(axis, 1 << i) for i in range(count.bit_length() - 1)]
    order = steps["lat"][:1] + steps["lon"][1:] + steps["lon"][:1] + steps["lat"][1:]
    other = jnp.zeros_like(value)
    for number, (axis, step) in enumerate(order):
        value = value if number == 0 else value + other
        other = lax.ppermute(value, axis, [(i, i ^ step) for i in range(lax.axis_size(axis))])
    return value, other


def whole_step(
    latent, gain_first, triple_first, output_first, gain_merge, merge_weight, gain_second, triple_second,
    output_second, split_weight,
):
    levels, height, width, channels = latent.shape
    wide = merge_weight.shape[1]
    plan = Plan(levels, height, width)
    maps = Maps()
    lat_count, lon_count = lax.axis_size("lat"), lax.axis_size("lon")

    def moved(value, lat_step, lon_step):
        pairs = [
            (a * lon_count + b, (a + lat_step) % lat_count * lon_count + (b + lon_step) % lon_count)
            for a in range(lat_count)
            for b in range(lon_count)
        ]
        return lax.ppermute(value, ("lat", "lon"), pairs)

    all_parts = sum(plan.parts, [])
    maps.add("own", sum(plan.blocks, []), all_parts)
    maps.add("ahead", sum(plan.results.values(), []), all_parts)
    cells = [
        (2 * r + ro, 2 * c + co)
        for ro in range(2)
        for co in range(2)
        for r in range(plan.coarse_rows)
        for c in range(plan.coarse_cols)
    ]
    half_rows, half_cols = height // 2, width // 2
    quarters = [
        (qr * half_rows + r, qc * half_cols + c)
        for qr in range(2)
        for qc in range(2)
        for r in range(half_rows)
        for c in range(half_cols)
    ]
    maps.add("quarters", cells, quarters)
    placed = [((r + half_rows) % height, (c + half_cols) % width) for r, c in quarters]
    maps.add("output", placed, plan.own)
    table, keys = maps.array(), maps.keys

    vmem = pl.BlockSpec(memory_space=pltpu.VMEM)
    smem = pl.BlockSpec(memory_space=pltpu.SMEM)
    bf16 = jnp.bfloat16

    def call(body, outs, args, scratch=(), flops=0, limit=16, specs=None):
        size = sum(math.prod(a.shape) * a.dtype.itemsize for a in args)
        return pl.pallas_call(
            body,
            out_shape=[jax.ShapeDtypeStruct(s, d) for s, d in outs],
            in_specs=specs or [smem if a.ndim == 1 else vmem for a in args],
            out_specs=[vmem] * len(outs),
            scratch_shapes=list(scratch),
            cost_estimate=pl.CostEstimate(flops=flops, bytes_accessed=size, transcendentals=0),
            compiler_params=pltpu.CompilerParams(vmem_limit_bytes=limit << 20),
        )(*args)

    def rows_of(*counts):
        return [((n, channels), bf16) for n in counts]

    count = plan.window
    x = latent.reshape(levels * height * width, channels)
    lat_index = lax.axis_index("lat").astype(jnp.int32)
    edge = (lat_index == lat_count - 1).astype(jnp.int32).reshape(1)
    n_block = plan.groups * count
    n_coarse = levels * len(plan.parts[0])
    n_part = len(plan.parts)
    n_sent = sent_sizes(plan)

    hbm = pl.BlockSpec(memory_space=pltpu.HBM)
    margin = -(-HALF_LON // 8) * 8
    s_lat, s_diag, s_lon = call(
        functools.partial(pack_kernel, plan),
        rows_of(*[levels * len(cells) for cells in plan.raw.values()]), (latent,),
        [
            pltpu.VMEM((levels, HALF_LAT, width, channels), bf16),
            pltpu.VMEM((levels, height - HALF_LAT, margin, channels), bf16),
            pltpu.SemaphoreType.DMA((2,)),
        ],
        flops=10**9, limit=LIMITS["pack"], specs=[hbm],
    )
    r_lat = moved(s_lat, -1, 0)
    r_diag = moved(s_diag, -1, -1)
    r_lon = moved(s_lon, 0, -1)
    gain1 = gain_first.reshape(1, channels)
    y_first, x_right, x_below, x_last, s_lat, s_lon, s_diag, bias = call(
        functools.partial(fine_first_kernel, plan),
        rows_of(n_block, *[n_block] * (len(plan.windows) - 1), *n_sent)
        + [((2 * plan.groups, count, count), jnp.float32)],
        (edge, x, gain1, triple_first, output_first),
        [
            pltpu.VMEM((n_block, 3 * channels), bf16),
            pltpu.VMEM((n_block, channels), bf16),
            pltpu.VMEM((n_block, channels), jnp.float32),
        ],
        flops=4 * 10**9, limit=LIMITS["first"],
    )
    fine_scratch = [
        pltpu.VMEM((n_block, channels), jnp.float32),
        pltpu.VMEM((n_block, 3 * channels), bf16),
        pltpu.VMEM((n_block, channels), bf16),
    ]
    fine_weights = (gain1, triple_first, output_first)

    def fine_edge(w, direction, sent, rest, raws):
        return call(
            functools.partial(fine_edge_kernel, plan, w, direction, list(raws)),
            rows_of(n_block, sent.shape[0]), (bias, sent, rest, *raws.values(), *fine_weights),
            fine_scratch, flops=2 * 10**9, limit=LIMITS["edge"],
        )

    y_right, s_lat = fine_edge(1, "res_lat", s_lat, x_right, {"raw_lon": r_lon})
    q_lat = moved(s_lat, -1, 0)
    q_diag = moved(s_diag, -1, -1)
    y_below, s_lon = fine_edge(2, "res_lon", s_lon, x_below, {"raw_lat": r_lat})
    q_lon = moved(s_lon, 0, -1)
    (parts,) = call(
        functools.partial(coarse_own_kernel, plan, keys, [len(plan.windows) - 1]),
        rows_of(n_part * n_coarse),
        (table, bias, y_first, y_right, y_below, x_last, r_lat, r_diag, r_lon, *fine_weights),
        [pltpu.VMEM((n_block, channels), bf16)] + fine_scratch, flops=4 * 10**9, limit=LIMITS["own"],
    )
    total_rows, total_cols = height * lat_count, width * lon_count
    angle = np.pi * ((np.arange(total_rows) + 0.5) / total_rows - 0.5)
    every = np.cos(angle)
    scaled = every / np.sqrt(total_cols * np.sum(every * every))
    frame_rows = np.array([[r for r, _ in plan.parts[2 * ro]] * levels for ro in range(2)])
    row_of = (np.arange(lat_count)[:, None, None] * height + frame_rows) % total_rows
    weights = jnp.asarray(scaled[row_of], jnp.float32)
    fine, upper, sums = call(
        functools.partial(coarse_kernel, plan, keys),
        rows_of(n_part * n_coarse) + [((n_coarse, wide), bf16), ((levels, channels), jnp.float32)],
        (
            table, bias, parts, q_lat, q_lon, q_diag, gain_merge.reshape(1, -1), merge_weight,
            gain_second.reshape(1, -1), triple_second, output_second, split_weight, lat_index.reshape(1), weights,
        ),
        [pltpu.VMEM((n_coarse, 3 * wide), bf16), pltpu.VMEM((n_coarse, wide), bf16)],
        flops=8 * 10**9, limit=LIMITS["coarse"],
    )
    own, s_lat, s_lon, s_diag = call(
        functools.partial(split_kernel, plan, keys), rows_of(*[n_coarse] * 4),
        (table, fine, upper, split_weight), [pltpu.VMEM((levels, n_part * n_coarse // levels, channels), bf16)],
        flops=2 * 10**9, limit=LIMITS["split"],
    )
    d_lat, d_lon, d_diag = (moved(s_lat, 1, 0), moved(s_lon, 0, 1), moved(s_diag, 1, 1))
    sums, other_sums = all_but_summed(sums)
    decoded, means = call(
        functools.partial(output_kernel, plan, keys),
        rows_of(levels * height * width) + [((levels, channels), jnp.float32)],
        (table, own, d_lon, d_lat, d_diag, sums, other_sums), flops=10**9, limit=LIMITS["output"],
    )
    return decoded.reshape(latent.shape), means


def solution(mesh):
    return jax.shard_map(
        whole_step,
        mesh=mesh,
        in_specs=(P(None, "lat", "lon", None), P(), P(), P(), P(), P(), P(), P(), P(), P()),
        out_specs=(P(None, "lat", "lon", None), P()),
        check_vma=False,
    )
```

```python
import functools
import math

import jax
import jax.numpy as jnp
import numpy as np
from jax import lax
from jax.experimental import pallas as pl
from jax.experimental.pallas import tpu as pltpu
from jax.sharding import PartitionSpec as P

HD = 64
WIN_LEV = 2
WIN_LAT = 6
WIN_LON = 12
HALF_LAT = WIN_LAT // 2
HALF_LON = WIN_LON // 2
LANES = 128

epsilon = 1e-05
masked_score = -1e30
score_scale = HD**-0.5 * math.log2(math.e)

LIMITS = {"pack": 59, "first": 16, "edge": 16, "own": 12, "coarse": 16, "split": 8, "output": 8}


class Plan:
    def __init__(self, levels, height, width):
        self.levels, self.height, self.width = levels, height, width
        assert levels % WIN_LEV == 0
        assert height == 2 * WIN_LAT and width == 2 * WIN_LON
        self.groups = levels // WIN_LEV
        half_lev = WIN_LEV // 2
        self.group_levels = [
            [(g * WIN_LEV + half_lev + i) % levels for i in range(WIN_LEV)] for g in range(self.groups)
        ]
        self.order = [lv for group in self.group_levels for lv in group]
        ids = [(((lv + half_lev)) // WIN_LEV) for lv in range(levels)]
        self.group_split = [len({ids[lv] for lv in group}) > 1 for group in self.group_levels]
        self.window = WIN_LEV * WIN_LAT * WIN_LON
        self.windows = [(wr, wc) for wr in range(height // WIN_LAT) for wc in range(width // WIN_LON)]

        self.blocks = [
            cells_of(
                (HALF_LAT + wr * WIN_LAT, HALF_LAT + (wr + 1) * WIN_LAT),
                (HALF_LON + wc * WIN_LON, HALF_LON + (wc + 1) * WIN_LON),
            )
            for wr, wc in self.windows
        ]
        self.own = cells_of((0, height), (0, width))
        fl, fc, fh, fw = HALF_LAT, HALF_LON, height, width
        self.raw = {
            "raw_lat": cells_of((fh, fh + fl), (fc, fw)),
            "raw_diag": cells_of((fh, fh + fl), (fw, fw + fc)),
            "raw_lon": cells_of((fl, fh), (fw, fw + fc)),
        }
        self.results = {
            "res_lat": padded(cells_of((fh + fl, fh + 2 * fl), (2 * fc, fw + fc))),
            "res_lon": padded(cells_of((2 * fl, fh + fl), (fw + fc, fw + 2 * fc))),
            "res_diag": padded(cells_of((fh + fl, fh + 2 * fl), (fw + fc, fw + 2 * fc))),
        }
        self.coarse_rows, self.coarse_cols = height // 2, width // 2
        self.parts = [
            [
                (2 * fl + 2 * r + ro, 2 * fc + 2 * c + co)
                for r in range(self.coarse_rows)
                for c in range(self.coarse_cols)
            ]
            for ro in range(2)
            for co in range(2)
        ]


def cells_of(rows, cols):
    return [(r, c) for r in range(*rows) for c in range(*cols)]


def padded(cells):
    return cells + [None] * (-len(cells) % 8)


def shifted(cells, rows, cols):
    return [cell and (cell[0] - rows, cell[1] - cols) for cell in cells]


def scatter_map(source, target):
    place = {cell: i for i, cell in enumerate(target) if cell is not None}
    return np.array([-1 if cell is None else place.get(cell, -1) for cell in source], np.int32)


class Maps:
    def __init__(self):
        self.rows, self.keys = [], {}

    def add(self, key, source, target):
        self.keys[key] = (len(self.rows), len(source), len(target))
        self.rows.append(scatter_map(source, target))

    def array(self):
        width = -(-max(len(v) for v in self.rows) // LANES) * LANES
        height = -(-len(self.rows) // 8) * 8
        out = np.full((height, width), -1, np.int32)
        for i, v in enumerate(self.rows):
            out[i, : len(v)] = v
        return jnp.asarray(out)


def table_hot(maps_ref, key):
    row, count, out_rows = key
    return one_hot(maps_ref[row : row + 1, :count], out_rows)


def one_hot(index, out_rows):
    hot = lax.broadcasted_iota(jnp.int32, (out_rows, index.shape[1]), 0) == index
    return jnp.where(hot, 1.0, 0.0).astype(jnp.bfloat16)


def box_hot(levels, rows, cols, boxes, out_rows, turn=0):
    token = lax.broadcasted_iota(jnp.int32, (1, levels * rows * cols), 1)

    def divided(value, by):
        return jnp.floor((value.astype(jnp.float32) + 0.5) * (1.0 / by)).astype(jnp.int32)

    level = divided(token, rows * cols)
    inner = token - level * (rows * cols)
    row = divided(inner, cols)
    col = inner - row * cols
    slot = jnp.where(level >= turn, level - turn, level + levels - turn)
    place = jnp.full_like(token, -1)
    for r0, r1, c0, c1, base, level_step, row_step in boxes:
        inside = (row >= r0) & (row < r1) & (col >= c0) & (col < c1)
        place = jnp.where(inside, base + slot * level_step + (row - r0) * row_step + (col - c0), place)
    return one_hot(place, out_rows)


def moved_rows(hot, source):
    return jnp.dot(hot, source, preferred_element_type=jnp.float32)


def normed_rows(value, gain):
    mean = jnp.mean(value, -1, keepdims=True)
    centred = value - mean
    var = jnp.mean(centred * centred, -1, keepdims=True)
    return (centred * lax.rsqrt(var + epsilon) * gain).astype(jnp.bfloat16)


def score_bias(count, group_split, edge):
    span = count // WIN_LEV
    rows = lax.broadcasted_iota(jnp.int32, (count, count), 0)
    cols = lax.broadcasted_iota(jnp.int32, (count, count), 1)
    q_lev, k_lev = rows >= span, cols >= span
    q_in = rows - jnp.where(q_lev, span, 0)
    k_in = cols - jnp.where(k_lev, span, 0)
    half = span // 2
    apart = (q_in >= half) != (k_in >= half)
    apart = jnp.where(apart, edge, 0)
    if group_split:
        apart = jnp.where(q_lev != k_lev, 1, apart)
    return jnp.where(apart > 0, masked_score, 0.0)


def head_pair(q, k, v, bias, low, high):
    trans = (((1,), (1,)), ((), ()))
    outs = []
    for keep, fill in ((low, high), (high, low)):
        s = lax.dot_general(q, k * keep, trans, preferred_element_type=jnp.float32)
        if bias is not None:
            s = s + bias
        peak = jnp.max(s, -1, keepdims=True)
        p = jnp.exp2((s - peak) * score_scale).astype(jnp.bfloat16)
        outs.append(jnp.dot(p, v * keep + fill, preferred_element_type=jnp.float32))
    is_low = lax.broadcasted_iota(jnp.int32, outs[0].shape, 1) < HD
    top = jnp.where(is_low, outs[0], outs[1])
    bottom = pltpu.roll(jnp.where(is_low, outs[1], outs[0]), HD, 1)
    return (top / bottom).astype(jnp.bfloat16)


def lane_masks():
    lane = lax.broadcasted_iota(jnp.int32, (1, LANES), 1)
    low = jnp.where(lane < HD, 1.0, 0.0).astype(jnp.bfloat16)
    high = jnp.where(lane < HD, 0.0, 1.0).astype(jnp.bfloat16)
    return low, high


def block_attention(qkv, att, row, channels, pair, bias, count):
    low, high = lane_masks()
    rows = pl.ds(row, count)
    base = pair * LANES

    def lanes(offset):
        start = base + offset
        return pl.ds(start if isinstance(start, int) else pl.multiple_of(start, LANES), LANES)

    q = qkv[rows, lanes(0)]
    k = qkv[rows, lanes(channels)]
    v = qkv[rows, lanes(2 * channels)]
    att[rows, lanes(0)] = head_pair(q, k, v, bias, low, high)


def split_rows(out_refs, value):
    start = 0
    for out in out_refs:
        out[...] = value[start : start + out.shape[0]].astype(out.dtype)
        start += out.shape[0]


def pack_kernel(plan, x_hbm, lat_ref, diag_ref, lon_ref, near_ref, far_ref, sems):
    levels, height, width = plan.levels, plan.height, plan.width
    fl, fc = HALF_LAT, HALF_LON
    copies = [
        pltpu.make_async_copy(x_hbm.at[:, 0:fl], near_ref, sems.at[0]),
        pltpu.make_async_copy(x_hbm.at[:, fl:height, 0 : far_ref.shape[2]], far_ref, sems.at[1]),
    ]
    for copy in copies:
        copy.start()
    turn = WIN_LEV // 2
    across, down = width - fc, height - fl
    lat_size, diag_size = lat_ref.shape[0], diag_ref.shape[0]
    near = box_hot(
        levels, fl, width,
        [(0, fl, fc, width, 0, fl * across, across), (0, fl, 0, fc, lat_size, fl * fc, fc)],
        lat_size + diag_size, turn,
    )
    far = box_hot(levels, down, far_ref.shape[2], [(0, down, 0, fc, 0, down * fc, fc)], lon_ref.shape[0], turn)
    channels = x_hbm.shape[-1]
    copies[0].wait()
    split_rows((lat_ref, diag_ref), moved_rows(near, near_ref[...].reshape(-1, channels)))
    copies[1].wait()
    lon_ref[...] = moved_rows(far, far_ref[...].reshape(-1, channels)).astype(lon_ref.dtype)


def fine_first_kernel(
    plan, edge_ref, x_ref, gain_ref, w_ref, wo_ref, y_ref, *more
):
    rest_refs, (slat_ref, slon_ref, sdiag_ref, bias, qkv, att, tokens_ref) = more[:-7], more[-7:]
    channels = x_ref.shape[1]
    levels, height, width = plan.levels, plan.height, plan.width
    fl, fc = HALF_LAT, HALF_LON
    count = plan.window
    area = WIN_LAT * WIN_LON

    def level_hot(rows):
        boxes = [
            (0, rows, fc, fc + WIN_LON, 0, 0, WIN_LON),
            (0, rows, fc + WIN_LON, width, area, 0, WIN_LON),
        ]
        return box_hot(1, rows, width, boxes, 2 * area)

    split_row = fl + WIN_LAT
    top_hot, bottom_hot = level_hot(WIN_LAT), level_hot(height - split_row)
    right_ref, below_ref, last_ref = rest_refs
    for i, lv in enumerate(plan.order):
        start = lv * height * width
        rows = slice(i * area, (i + 1) * area)
        top = moved_rows(top_hot, x_ref[start + fl * width : start + split_row * width, :])
        tokens_ref[rows, :] = top[:area]
        right_ref[rows, :] = top[area:].astype(jnp.bfloat16)
        bottom = moved_rows(bottom_hot, x_ref[start + split_row * width : start + height * width, :])
        below_ref[rows, :] = bottom[:area].astype(jnp.bfloat16)
        last_ref[rows, :] = bottom[area:].astype(jnp.bfloat16)
    tokens = tokens_ref[...]
    normed = normed_rows(tokens, gain_ref[...])
    qkv[...] = jnp.dot(normed, w_ref[...], preferred_element_type=jnp.float32).astype(jnp.bfloat16)
    for g in range(plan.groups):
        bias[2 * g] = score_bias(count, plan.group_split[g], 0)
        bias[2 * g + 1] = score_bias(count, plan.group_split[g], edge_ref[0])
    for pair in range(channels // LANES):
        for g in range(plan.groups):
            b = bias[2 * g] if plan.group_split[g] else None
            block_attention(qkv, att, g * count, channels, pair, b, count)
    update = jnp.dot(att[...], wo_ref[...], preferred_element_type=jnp.float32)
    y = (tokens + update).astype(jnp.bfloat16)
    y_ref[...] = y
    hot = sent_hot(plan, 0)
    for i in range(levels):
        moved = moved_rows(hot, y_ref[i * area : (i + 1) * area, :]).astype(jnp.bfloat16)
        start = 0
        for out in (slat_ref, slon_ref, sdiag_ref):
            size = out.shape[0] // levels
            out[i * size : (i + 1) * size, :] = moved[start : start + size]
            start += size


def sent_sizes(plan):
    return [plan.levels * len(cells) for cells in plan.results.values()]


def sent_hot(plan, w, only=None):
    boxes, start = [], 0
    shifts = {"res_lat": (plan.height, 0), "res_lon": (0, plan.width), "res_diag": (plan.height, plan.width)}
    for name, cells in plan.results.items():
        sent = [cell for cell in shifted(cells, *shifts[name]) if cell is not None]
        r0, c0 = sent[0]
        r1, c1 = sent[-1]
        w0, v0 = plan.blocks[w][0]
        top, left = max(r0, w0), max(c0, v0)
        bottom, right = min(r1 + 1, w0 + WIN_LAT), min(c1 + 1, v0 + WIN_LON)
        if top < bottom and left < right and only in (None, name):
            row_step = c1 + 1 - c0
            base = start + (top - r0) * row_step + (left - c0)
            boxes.append((top - w0, bottom - w0, left - v0, right - v0, base, len(cells), row_step))
        if only is None:
            start += len(cells)
    out_rows = start if only is None else len(plan.results[only])
    return box_hot(1, WIN_LAT, WIN_LON, boxes, out_rows)


def raw_hot(plan, name, w, out_rows):
    cells = plan.raw[name]
    (r0, c0), (r1, c1) = cells[0], cells[-1]
    w0, v0 = plan.blocks[w][0]
    top, left = max(r0, w0), max(c0, v0)
    bottom, right = min(r1 + 1, w0 + WIN_LAT), min(c1 + 1, v0 + WIN_LON)
    if not (top < bottom and left < right):
        return None
    base = (top - w0) * WIN_LON + (left - v0)
    box = (top - r0, bottom - r0, left - c0, right - c0, base, WIN_LAT * WIN_LON, WIN_LON)
    return box_hot(plan.levels, r1 + 1 - r0, c1 + 1 - c0, [box], out_rows)


def fine_windows(plan, which, bias, rest_ref, raw, gain_ref, w_ref, wo_ref, y_ref, tokens, qkv, att):
    channels = rest_ref.shape[1]
    count = plan.window
    block = plan.groups * count
    for i, w in enumerate(which):
        value = rest_ref[i * block : (i + 1) * block, :].astype(jnp.float32)
        for name, ref in raw.items():
            hot = raw_hot(plan, name, w, block)
            if hot is not None:
                value = value + moved_rows(hot, ref[...])
        tokens[i * block : (i + 1) * block, :] = value
    normed = normed_rows(tokens[...], gain_ref[...])
    qkv[...] = jnp.dot(normed, w_ref[...], preferred_element_type=jnp.float32).astype(jnp.bfloat16)

    def window(i, below):
        for pair in range(channels // LANES):
            for g in range(plan.groups):
                row = i * block + g * count
                if not isinstance(row, int):
                    row = pl.multiple_of(row, 16)
                block_attention(qkv, att, row, channels, pair, bias[2 * g + below], count)

    belows = [plan.windows[w][0] for w in which]
    if len(which) == 1:
        window(0, belows[0])
    else:
        assert belows == list(range(len(which)))

        @pl.loop(0, len(which))
        def _(i):
            window(i, i)

    update = jnp.dot(att[...], wo_ref[...], preferred_element_type=jnp.float32)
    y = (tokens[...] + update).astype(jnp.bfloat16)
    y_ref[...] = y
    return y


def fine_edge_kernel(plan, w, name, raw_names, bias, sent_ref, rest_ref, last_ref, *more):
    raw = dict(zip(raw_names, more))
    gain_ref, w_ref, wo_ref, y_ref, out_ref, last_out_ref, tokens, qkv, att = more[len(raw_names) :]
    last = last_ref[...].astype(jnp.float32)
    for raw_name, ref in raw.items():
        last = last + moved_rows(raw_hot(plan, raw_name, len(plan.windows) - 1, last.shape[0]), ref[...])
    last_out_ref[...] = last.astype(jnp.bfloat16)
    fine_windows(plan, [w], bias, rest_ref, raw, gain_ref, w_ref, wo_ref, y_ref, tokens, qkv, att)
    hot = sent_hot(plan, w, name)
    area, size = WIN_LAT * WIN_LON, out_ref.shape[0] // plan.levels
    for i in range(plan.levels):
        rows = slice(i * size, (i + 1) * size)
        moved = moved_rows(hot, y_ref[i * area : (i + 1) * area, :])
        out_ref[rows, :] = (sent_ref[rows, :].astype(jnp.float32) + moved).astype(jnp.bfloat16)


def coarse_own_kernel(
    plan, keys, which, maps_ref, bias, first_ref, right_ref, below_ref, rest_ref, diag_hbm, gain_ref, w_ref,
    wo_ref, part_ref, y_ref, tokens, qkv, att, diag_ref, sem,
):
    copy = pltpu.make_async_copy(diag_hbm, diag_ref, sem)
    copy.start()
    area = WIN_LAT * WIN_LON
    parts = len(plan.parts)
    total = part_ref.shape[0] // parts
    hot = table_hot(maps_ref, keys["own"])
    for i in range(plan.levels):
        rows = slice(i * area, (i + 1) * area)
        stacked = jnp.concatenate([ref[rows, :] for ref in (first_ref, right_ref, below_ref)], 0)
        value = moved_rows(hot, stacked).astype(jnp.bfloat16)
        for k in range(parts):
            start = k * total + i * area
            part_ref[start : start + area, :] = value[k * area : (k + 1) * area]
    copy.wait()
    raw = {"raw_diag": diag_ref}
    fine_windows(plan, which, bias, rest_ref, raw, gain_ref, w_ref, wo_ref, y_ref, tokens, qkv, att)
    hot = table_hot(maps_ref, keys["own_last"])
    for i in range(plan.levels):
        value = moved_rows(hot, y_ref[i * area : (i + 1) * area, :])
        for k in range(parts):
            rows = slice(k * total + i * area, k * total + (i + 1) * area)
            early = part_ref[rows, :].astype(jnp.float32)
            part_ref[rows, :] = (early + value[k * area : (k + 1) * area]).astype(jnp.bfloat16)


def thirds(value):
    first = value.astype(jnp.bfloat16).astype(jnp.float32)
    second = (value - first).astype(jnp.bfloat16).astype(jnp.float32)
    return jnp.concatenate([first, second, value - first - second], 0).astype(jnp.bfloat16)


def summed_thirds(stacked, right):
    out = jnp.dot(stacked, right, preferred_element_type=jnp.float32)
    rows = out.shape[0] // 3
    return out[:rows] + out[rows : 2 * rows] + out[2 * rows :]


def coarse_kernel(
    plan, keys, maps_ref, bias, part_ref, lat_ref, lon_ref, diag_ref, gm_ref, wm_ref, gs_ref, ws_ref, wo_ref,
    wsp_ref, lat_index_ref, weight_ref, fine_ref, upper_ref, sums_ref, qkv, att,
):
    parts = len(plan.parts)
    channels = part_ref.shape[1]
    total = upper_ref.shape[0]
    wide = ws_ref.shape[0]
    count = plan.window
    levels = plan.levels
    area = total // levels
    hot = table_hot(maps_ref, keys["ahead"])
    for i in range(levels):
        pieces = []
        for ref in (lat_ref, lon_ref, diag_ref):
            size = ref.shape[0] // levels
            pieces.append(ref[i * size : (i + 1) * size, :])
        value = moved_rows(hot, jnp.concatenate(pieces, 0))
        for k in range(parts):
            rows = slice(k * total + i * area, k * total + (i + 1) * area)
            own = part_ref[rows, :].astype(jnp.float32)
            fine_ref[rows, :] = (own + value[k * area : (k + 1) * area]).astype(jnp.bfloat16)

    def part(k):
        return fine_ref[k * total : (k + 1) * total, :].astype(jnp.float32)

    mean = sum(jnp.sum(part(k), -1, keepdims=True) for k in range(parts)) / (parts * channels)
    square = sum(jnp.sum((part(k) - mean) ** 2, -1, keepdims=True) for k in range(parts))
    scale = lax.rsqrt(square / (parts * channels) + epsilon)
    merged = 0.0
    for k in range(parts):
        span = slice(k * channels, (k + 1) * channels)
        normed = ((part(k) - mean) * scale * gm_ref[:, span]).astype(jnp.bfloat16)
        merged = merged + jnp.dot(normed, wm_ref[span, :], preferred_element_type=jnp.float32)
    coarse = merged.astype(jnp.bfloat16).astype(jnp.float32)
    normed = normed_rows(coarse, gs_ref[...])
    qkv[...] = jnp.dot(normed, ws_ref[...], preferred_element_type=jnp.float32).astype(jnp.bfloat16)

    at_once = 8

    @pl.loop(0, wide // LANES // at_once)
    def _(step):
        for i in range(at_once):
            for g in range(plan.groups):
                block_attention(qkv, att, g * count, wide, step * at_once + i, bias[2 * g + 1], count)

    update = jnp.dot(att[...], wo_ref[...], preferred_element_type=jnp.float32)
    upper = (coarse + update).astype(jnp.bfloat16)
    upper_ref[...] = upper
    span = total // levels
    token = lax.broadcasted_iota(jnp.int32, (levels, total), 1)
    level = lax.broadcasted_iota(jnp.int32, (levels, total), 0)
    inside = (token >= level * span) & (token < (level + 1) * span)
    mine = weight_ref[lat_index_ref[0]]
    rows = jnp.concatenate([jnp.where(inside, mine[ro : ro + 1, :], 0.0) for ro in range(2)], 0)
    weights = thirds(rows)
    heavy = thirds(summed_thirds(weights, upper))
    spread = summed_thirds(heavy, wsp_ref[...])
    sums = 0.0
    for k in range(parts):
        ro = k // 2
        fine = summed_thirds(weights, fine_ref[k * total : (k + 1) * total, :])
        sums = sums + (fine + spread[:, k * channels : (k + 1) * channels])[ro * levels : (ro + 1) * levels]
    for i, lv in enumerate(plan.order):
        sums_ref[lv : lv + 1, :] = sums[i : i + 1]


def split_kernel(plan, keys, maps_ref, fine_ref, upper_ref, wsp_ref, own_ref, slat_ref, slon_ref, sdiag_ref, decoded):
    parts = len(plan.parts)
    total = upper_ref.shape[0]
    channels = fine_ref.shape[1]
    levels = plan.levels
    span = total // levels
    upper = upper_ref[...]
    for k in range(parts):
        spread = jnp.dot(upper, wsp_ref[:, k * channels : (k + 1) * channels], preferred_element_type=jnp.float32)
        value = (fine_ref[k * total : (k + 1) * total, :].astype(jnp.float32) + spread).astype(jnp.bfloat16)
        for i in range(levels):
            decoded[i, k * span : (k + 1) * span, :] = value[i * span : (i + 1) * span]
    quarter = parts * (span // 4)
    hot = table_hot(maps_ref, keys["quarters"])
    for i in range(levels):
        moved = jnp.dot(hot, decoded[i], preferred_element_type=jnp.float32).astype(jnp.bfloat16)
        for q, out in enumerate((own_ref, slon_ref, slat_ref, sdiag_ref)):
            out[i * quarter : (i + 1) * quarter, :] = moved[q * quarter : (q + 1) * quarter]


def output_kernel(plan, keys, maps_ref, own_ref, lon_ref, lat_ref, diag_ref, out_ref):
    span = own_ref.shape[0] // plan.levels
    tile = plan.height * plan.width
    hot = table_hot(maps_ref, keys["output"])
    for i, lv in enumerate(plan.order):
        rows = slice(i * span, (i + 1) * span)
        stacked = jnp.concatenate(
            [ref[rows, :].astype(jnp.float32) for ref in (own_ref, lon_ref, lat_ref, diag_ref)], 0
        ).astype(jnp.bfloat16)
        moved = jnp.dot(hot, stacked, preferred_element_type=jnp.float32)
        out_ref[lv * tile : (lv + 1) * tile, :] = moved.astype(jnp.bfloat16)


def all_but_summed(value):
    steps = {}
    for axis in ("lat", "lon"):
        count = lax.axis_size(axis)
        assert count & (count - 1) == 0
        steps[axis] = [(axis, 1 << i) for i in range(count.bit_length() - 1)]
    order = steps["lat"][:1] + steps["lon"][1:] + steps["lon"][:1] + steps["lat"][1:]
    other = jnp.zeros_like(value)
    for number, (axis, step) in enumerate(order):
        value = value if number == 0 else value + other
        other = lax.ppermute(value, axis, [(i, i ^ step) for i in range(lax.axis_size(axis))])
    return value, other


def whole_step(
    latent, gain_first, triple_first, output_first, gain_merge, merge_weight, gain_second, triple_second,
    output_second, split_weight,
):
    levels, height, width, channels = latent.shape
    wide = merge_weight.shape[1]
    plan = Plan(levels, height, width)
    maps = Maps()
    lat_count, lon_count = lax.axis_size("lat"), lax.axis_size("lon")

    def moved(value, lat_step, lon_step):
        pairs = [
            (a * lon_count + b, (a + lat_step) % lat_count * lon_count + (b + lon_step) % lon_count)
            for a in range(lat_count)
            for b in range(lon_count)
        ]
        return lax.ppermute(value, ("lat", "lon"), pairs)

    all_parts = sum(plan.parts, [])
    maps.add("own", sum(plan.blocks[:-1], []), all_parts)
    maps.add("own_last", plan.blocks[-1], all_parts)
    maps.add("ahead", sum(plan.results.values(), []), all_parts)
    cells = [
        (2 * r + ro, 2 * c + co)
        for ro in range(2)
        for co in range(2)
        for r in range(plan.coarse_rows)
        for c in range(plan.coarse_cols)
    ]
    half_rows, half_cols = height // 2, width // 2
    quarters = [
        (qr * half_rows + r, qc * half_cols + c)
        for qr in range(2)
        for qc in range(2)
        for r in range(half_rows)
        for c in range(half_cols)
    ]
    maps.add("quarters", cells, quarters)
    placed = [((r + half_rows) % height, (c + half_cols) % width) for r, c in quarters]
    maps.add("output", placed, plan.own)
    table, keys = maps.array(), maps.keys

    vmem = pl.BlockSpec(memory_space=pltpu.VMEM)
    smem = pl.BlockSpec(memory_space=pltpu.SMEM)
    bf16 = jnp.bfloat16

    def call(body, outs, args, scratch=(), flops=0, limit=16, specs=None):
        size = sum(math.prod(a.shape) * a.dtype.itemsize for a in args)
        return pl.pallas_call(
            body,
            out_shape=[jax.ShapeDtypeStruct(s, d) for s, d in outs],
            in_specs=specs or [smem if a.ndim == 1 else vmem for a in args],
            out_specs=[vmem] * len(outs),
            scratch_shapes=list(scratch),
            cost_estimate=pl.CostEstimate(flops=flops, bytes_accessed=size, transcendentals=0),
            compiler_params=pltpu.CompilerParams(vmem_limit_bytes=limit << 20),
        )(*args)

    def rows_of(*counts):
        return [((n, channels), bf16) for n in counts]

    count = plan.window
    x = latent.reshape(levels * height * width, channels)
    lat_index = lax.axis_index("lat").astype(jnp.int32)
    edge = (lat_index == lat_count - 1).astype(jnp.int32).reshape(1)
    n_block = plan.groups * count
    n_coarse = levels * len(plan.parts[0])
    n_part = len(plan.parts)
    n_sent = sent_sizes(plan)

    hbm = pl.BlockSpec(memory_space=pltpu.HBM)
    margin = -(-HALF_LON // 8) * 8
    s_lat, s_diag, s_lon = call(
        functools.partial(pack_kernel, plan),
        rows_of(*[levels * len(cells) for cells in plan.raw.values()]), (latent,),
        [
            pltpu.VMEM((levels, HALF_LAT, width, channels), bf16),
            pltpu.VMEM((levels, height - HALF_LAT, margin, channels), bf16),
            pltpu.SemaphoreType.DMA((2,)),
        ],
        flops=10**9, limit=LIMITS["pack"], specs=[hbm],
    )
    r_lat = moved(s_lat, -1, 0)
    r_diag = moved(s_diag, -1, -1)
    r_lon = moved(s_lon, 0, -1)
    gain1 = gain_first.reshape(1, channels)
    y_first, x_right, x_below, x_last, s_lat, s_lon, s_diag, bias = call(
        functools.partial(fine_first_kernel, plan),
        rows_of(n_block, *[n_block] * (len(plan.windows) - 1), *n_sent)
        + [((2 * plan.groups, count, count), jnp.float32)],
        (edge, x, gain1, triple_first, output_first),
        [
            pltpu.VMEM((n_block, 3 * channels), bf16),
            pltpu.VMEM((n_block, channels), bf16),
            pltpu.VMEM((n_block, channels), jnp.float32),
        ],
        flops=4 * 10**9, limit=LIMITS["first"],
    )
    fine_scratch = [
        pltpu.VMEM((n_block, channels), jnp.float32),
        pltpu.VMEM((n_block, 3 * channels), bf16),
        pltpu.VMEM((n_block, channels), bf16),
    ]
    fine_weights = (gain1, triple_first, output_first)

    def fine_edge(w, direction, sent, rest, last, raws):
        return call(
            functools.partial(fine_edge_kernel, plan, w, direction, list(raws)),
            rows_of(n_block, sent.shape[0], n_block), (bias, sent, rest, last, *raws.values(), *fine_weights),
            fine_scratch, flops=2 * 10**9, limit=LIMITS["edge"],
        )

    y_right, s_lat, x_last = fine_edge(1, "res_lat", s_lat, x_right, x_last, {"raw_lon": r_lon})
    q_lat = moved(s_lat, -1, 0)
    q_diag = moved(s_diag, -1, -1)
    y_below, s_lon, x_last = fine_edge(2, "res_lon", s_lon, x_below, x_last, {"raw_lat": r_lat})
    q_lon = moved(s_lon, 0, -1)
    (parts,) = call(
        functools.partial(coarse_own_kernel, plan, keys, [len(plan.windows) - 1]),
        rows_of(n_part * n_coarse),
        (table, bias, y_first, y_right, y_below, x_last, r_diag, *fine_weights),
        [pltpu.VMEM((n_block, channels), bf16), *fine_scratch, pltpu.VMEM(r_diag.shape, bf16), pltpu.SemaphoreType.DMA],
        flops=4 * 10**9, limit=LIMITS["own"], specs=[vmem] * 6 + [hbm] + [vmem] * len(fine_weights),
    )
    total_rows, total_cols = height * lat_count, width * lon_count
    angle = np.pi * ((np.arange(total_rows) + 0.5) / total_rows - 0.5)
    every = np.cos(angle)
    scaled = every / np.sqrt(total_cols * np.sum(every * every))
    frame_rows = np.array([[r for r, _ in plan.parts[2 * ro]] * levels for ro in range(2)])
    row_of = (np.arange(lat_count)[:, None, None] * height + frame_rows) % total_rows
    weights = jnp.asarray(scaled[row_of], jnp.float32)
    fine, upper, sums = call(
        functools.partial(coarse_kernel, plan, keys),
        rows_of(n_part * n_coarse) + [((n_coarse, wide), bf16), ((levels, channels), jnp.float32)],
        (
            table, bias, parts, q_lat, q_lon, q_diag, gain_merge.reshape(1, -1), merge_weight,
            gain_second.reshape(1, -1), triple_second, output_second, split_weight, lat_index.reshape(1), weights,
        ),
        [pltpu.VMEM((n_coarse, 3 * wide), bf16), pltpu.VMEM((n_coarse, wide), bf16)],
        flops=8 * 10**9, limit=LIMITS["coarse"],
    )
    own, s_lat, s_lon, s_diag = call(
        functools.partial(split_kernel, plan, keys), rows_of(*[n_coarse] * 4),
        (table, fine, upper, split_weight), [pltpu.VMEM((levels, n_part * n_coarse // levels, channels), bf16)],
        flops=2 * 10**9, limit=LIMITS["split"],
    )
    d_lat, d_lon, d_diag = (moved(s_lat, 1, 0), moved(s_lon, 0, 1), moved(s_diag, 1, 1))
    sums, other_sums = all_but_summed(sums)
    (decoded,) = call(
        functools.partial(output_kernel, plan, keys), rows_of(levels * height * width),
        (table, own, d_lon, d_lat, d_diag), flops=10**9, limit=LIMITS["output"],
    )
    return decoded.reshape(latent.shape), sums + other_sums


def solution(mesh):
    return jax.shard_map(
        whole_step,
        mesh=mesh,
        in_specs=(P(None, "lat", "lon", None), P(), P(), P(), P(), P(), P(), P(), P(), P()),
        out_specs=(P(None, "lat", "lon", None), P()),
        check_vma=False,
    )
```
